32 devices in a mesh: groups: 2 (over y), space: 4 (over z), dp: 2 (over x), ysp: 2 (over core).
Axes of the slice: x: 2, y: 2, z: 4, core: 2. Of those that a mesh axis runs over, the one named last changes fastest.
Arguments:
- inputs: bfloat16 [4, 8, 16, 2048], P(('groups', 'dp'), 'space', 'ysp'), parts along dimension 0, may hold values from -6 to 6
- w_first: float32 [864, 64], replicated, may hold values from -0.21875 to 0.21875
- b_first: float32 [64], replicated, may hold values from -2 to 2
- w_second: float32 [1728, 64], replicated, may hold values from -0.15625 to 0.15625
- b_second: float32 [64], replicated, may hold values from -2 to 2
- cotangent: bfloat16 [4, 8, 16, 4096], P(('groups', 'dp'), 'space', 'ysp'), parts along dimension 0, may hold values from -16 to 16
Outputs:
- output: bfloat16 [4, 8, 16, 4096], P(('groups', 'dp'), 'space', 'ysp'), parts along dimension 0
- input_grad: bfloat16 [4, 8, 16, 2048], P(('groups', 'dp'), 'space', 'ysp'), parts along dimension 0
- grad_w_first: float32 [1728, 64], P('groups'), parts along dimension 0
- grad_b_first: float32 [128], P('groups'), parts along dimension 0
- grad_w_second: float32 [3456, 64], P('groups'), parts along dimension 0
- grad_b_second: float32 [128], P('groups'), parts along dimension 0
The draws below stay inside these ranges and needn't reach their ends.
There are 2 independent parts, one for each index of `groups`. The reference program is written for one: setup_inputs(seed, part) draws one part's arguments, and reference() takes and returns one part's arrays. A program takes and returns all parts, laid end to end along the dimension named above; an argument that names none is the same for every part. Nothing has to cross between parts.
All inputs are finite; a program needn't handle non-finite values.
Results may differ from the reference program's by a relative error of at most 0.0075.
Values may be sent and summed in bfloat16 or wider, within the bound.
No kernel may reach another device: no remote copies, remote signals or barrier semaphores. Data moves between devices by JAX's collectives and lax.ppermute only.
A program may use at most 64 MiB of HBM per device.

```python
import jax
import jax.numpy as jnp
from jax import lax

C_IN = 32
C_MID = 64
DEPTH = 64
SAMPLES = 2
NX = 8
NY = 16


def draw_cotangent(key, part):
    shape = (SAMPLES, NX, NY, DEPTH * C_MID)
    ramp_x = 0.5 + jnp.arange(NX, dtype=jnp.float32) / max(NX - 1, 1)
    ramp_s = 0.5 + jnp.arange(SAMPLES, dtype=jnp.float32) / max(SAMPLES - 1, 1)
    ramp = ramp_s[:, None, None, None] * ramp_x[None, :, None, None]
    base = jax.random.truncated_normal(key, -4.0, 4.0, shape, jnp.float32)
    return (base * ramp).astype(jnp.bfloat16)


def level_of(own_key, extent, cuts, low, largest):
    loudness, own = 1.0, jax.random.fold_in(own_key, 6)
    for axis_at, shards_of in cuts:
        draws = jnp.exp(jax.random.uniform(jax.random.fold_in(own, axis_at), (shards_of,), jnp.float32, low / len(cuts), largest / len(cuts)))
        loudness = loudness * jnp.repeat(draws, extent[axis_at] // shards_of).reshape([-1 if axis == axis_at else 1 for axis in range(len(extent))])
    return loudness


def scatter_about(key, extent, width, most, pieces=(), kind=jnp.bfloat16):
    factor_of = level_of(key, extent, pieces, -0.22, 0.18) if pieces else 1.0
    array = jax.random.normal(key, extent, jnp.float32) * width * factor_of
    return jnp.minimum(jnp.maximum(array, -most), most).astype(kind)


def setup_inputs(seed: int = 0, part: int = 0) -> dict:
    keys = jax.random.split(jax.random.key(seed), 7)
    part_keys = jax.random.split(jax.random.fold_in(keys[6], part), 7)
    return {
        "inputs": scatter_about(part_keys[0], (SAMPLES, NX, NY, DEPTH * C_IN), 1.0, 6.0, ((0, 2), (1, 4), (2, 2))),
        "w_first": scatter_about(keys[1], (27 * C_IN, C_MID), (27 * C_IN) ** -0.5, 0.21875, (), jnp.float32),
        "b_first": scatter_about(keys[2], (C_MID,), 0.5, 2.0, (), jnp.float32),
        "w_second": scatter_about(keys[3], (27 * C_MID, C_MID), (27 * C_MID) ** -0.5, 0.15625, (), jnp.float32),
        "b_second": scatter_about(keys[4], (C_MID,), 0.5, 2.0, (), jnp.float32),
        "cotangent": draw_cotangent(jax.random.fold_in(jax.random.fold_in(keys[6], part), 71), part),
    }


def conv(field, weights):
    return lax.conv_general_dilated(field, weights, (1, 1, 1), 'SAME', dimension_numbers=('NDHWC', 'DHWIO', 'NDHWC'), precision=lax.Precision.HIGHEST)

def silu_grad(value):
    sig = jax.nn.sigmoid(value)
    return sig * (1.0 + value * (1.0 - sig))

def reference(inputs, w_first, b_first, w_second, b_second, cotangent):
    samples, nx_all, ny_all = (inputs.shape[0], inputs.shape[1], inputs.shape[2])
    x_cells = inputs.reshape(samples, nx_all, ny_all, DEPTH, C_IN).astype(jnp.float32)
    w1_round = lax.optimization_barrier(w_first.astype(jnp.bfloat16))
    w2_round = lax.optimization_barrier(w_second.astype(jnp.bfloat16))
    w1_cube = w1_round.astype(jnp.float32).reshape(3, 3, 3, C_IN, C_MID)
    w2_cube = w2_round.astype(jnp.float32).reshape(3, 3, 3, C_MID, C_MID)
    y_first = conv(x_cells, w1_cube) + b_first
    a_first = jax.nn.silu(y_first).astype(jnp.bfloat16).astype(jnp.float32)
    y_second = conv(a_first, w2_cube) + b_second
    output = jax.nn.silu(y_second).astype(jnp.bfloat16)
    cot_cells = cotangent.reshape(samples, nx_all, ny_all, DEPTH, C_MID).astype(jnp.float32)
    g_second = (cot_cells * silu_grad(y_second)).astype(jnp.bfloat16).astype(jnp.float32)
    unused_two, pull_second = jax.vjp(conv, a_first, w2_cube)
    d_first, grad_w2 = pull_second(g_second)
    grad_b2 = lax.optimization_barrier(jnp.sum(g_second, axis=(0, 1, 2, 3)))
    g_first = (d_first * silu_grad(y_first)).astype(jnp.bfloat16).astype(jnp.float32)
    unused_one, pull_first = jax.vjp(conv, x_cells, w1_cube)
    d_input, grad_w1 = pull_first(g_first)
    grad_b1 = lax.optimization_barrier(jnp.sum(g_first, axis=(0, 1, 2, 3)))
    out_flat = output.reshape(samples, nx_all, ny_all, DEPTH * C_MID)
    dx_flat = d_input.astype(jnp.bfloat16).reshape(samples, nx_all, ny_all, DEPTH * C_IN)
    return (out_flat, dx_flat, grad_w1.reshape(27 * C_IN, C_MID), grad_b1, grad_w2.reshape(27 * C_MID, C_MID), grad_b2)
```

```python
import jax
import jax.numpy as jnp
from jax import lax
from jax.experimental import pallas as pl
from jax.experimental.pallas import tpu as pltpu
from jax.sharding import PartitionSpec as P

C_IN = 32
C_MID = 64
DEPTH = 64
BF = jnp.bfloat16
F32 = jnp.float32
GROUP = 4
ROWS = DEPTH // GROUP
IN_L = GROUP * C_IN
MID_L = GROUP * C_MID
TAP1 = 3 * C_IN
TAP2 = 3 * C_MID
W1_L = 9 * TAP1
W2_L = 9 * TAP2
PACK2 = 1792
PACK1 = 896
NT = (((1,), (1,)), ((), ()))
NN = (((1,), (0,)), ((), ()))


def call(body, outs, scratch=(), vmem=40 << 20, cost=None):
    return pl.pallas_call(
        body,
        out_shape=[jax.ShapeDtypeStruct(shape, kind) for shape, kind in outs],
        scratch_shapes=list(scratch),
        compiler_params=pltpu.CompilerParams(vmem_limit_bytes=vmem),
        cost_estimate=cost,
    )


def dot(a, b, dims):
    return lax.dot_general(a, b, dims, preferred_element_type=F32)


def window(ref, start, width):
    frame = 256 if width <= 128 else 384
    at = start // 128 * 128
    value = ref[:, at : at + frame]
    if start != at:
        value = pltpu.roll(value, frame - (start - at), 1)
    lane = lax.broadcasted_iota(jnp.int32, value.shape, 1)
    return jnp.where(lane < width, value, 0.0)


def banded_body(w1_ref, w2_ref, f1_ref, f2_ref, r2_ref, r1_ref, pad1, pad2):
    pad1[...] = jnp.zeros(pad1.shape, F32)
    pad2[...] = jnp.zeros(pad2.shape, F32)
    pad1[:, :W1_L] = w1_ref[...]
    pad2[:, :W2_L] = w2_ref[...]
    for tap in range(9):
        one = window(pad1, tap * TAP1, TAP1)
        two = window(pad2, tap * TAP2, TAP2)
        for m in range(-1, 5):
            at = (m % 6) * C_MID
            s1 = pltpu.roll(one, ((m - 1) * C_IN) % 256, 1) if m != 1 else one
            s2 = pltpu.roll(two, ((m - 1) * C_MID) % 384, 1) if m != 1 else two
            s1 = s1.astype(BF)
            s2 = s2.astype(BF)
            if 0 <= m < 4:
                f1_ref[tap, m * C_MID : (m + 1) * C_MID, :] = s1
                f2_ref[tap, m * C_MID : (m + 1) * C_MID, :] = s2
            r1_ref[tap, at : at + C_MID, :] = s1[:, :IN_L]
            r2_ref[tap, at : at + C_MID, :] = s2[:, :MID_L]


def edges(value, low, high):
    count = value.shape[0]
    row = lax.broadcasted_iota(jnp.int32, (count, 128), 0) % ROWS
    lane = lax.broadcasted_iota(jnp.int32, (count, 128), 1)
    after = pltpu.roll(value[:, low : low + 128], count - 1, 0)
    before = pltpu.roll(value[:, high : high + 128], 1, 0)
    after = jnp.where(row == ROWS - 1, 0.0, after)
    before = jnp.where(row == 0, 0.0, before)
    return jnp.where(lane < 64, after, before)


def spread(planes, beside, core, to_ref, lanes):
    for x, plane in enumerate(planes):
        side = beside[x].astype(F32)
        low = jnp.where(core == 1, side, 0.0)
        high = jnp.where(core == 0, side, 0.0)
        cells = jnp.concatenate([low, plane.astype(F32), high], axis=0)
        rows = cells.reshape(-1, lanes)
        shape = cells.shape[:2]
        to_ref[x, :, :, :lanes] = cells.astype(BF)
        edge = edges(rows, 0, lanes - 128)
        to_ref[x, :, :, lanes:] = edge.astype(BF).reshape(*shape, 128)


def plane_mask(x, rows, space, last, core):
    row = lax.broadcasted_iota(jnp.int32, (rows, 1), 0)
    inside = jnp.float32(1.0)
    if x == 0:
        inside = jnp.where(space > 0, 1.0, 0.0)
    if x == 3:
        inside = jnp.where(space < last, 1.0, 0.0)
    low = jnp.where(core == 1, 1.0, 0.0)
    high = jnp.where(core == 0, 1.0, 0.0)
    mask = jnp.where(row < ROWS, low, jnp.where(row >= rows - ROWS, high, 1.0))
    return mask * inside


def forward_body(x_ref, l_ref, r_ref, y_ref, f1_ref, f2_ref, b1_ref, b2_ref, c_ref, e_ref, a_ref, d_ref, o_ref, g_ref, acc):
    core = lax.axis_index("ysp")
    space = lax.axis_index("space")
    last = lax.axis_size("space") - 1
    planes = [ref[i] for ref in (l_ref, x_ref, r_ref) for i in range(2)]
    spread(planes, y_ref, core, e_ref, IN_L)
    wide = x_ref.shape[1] + 2
    total = None
    for tap in range(9):
        a, b = divmod(tap, 3)
        part = dot(e_ref[a : a + 4, b : b + wide].reshape(-1, 256), f1_ref[tap], NT)
        total = part if total is None else total + part
    acc[...] = total
    rows = wide * ROWS
    for x in range(4):
        y1 = acc[x * rows : (x + 1) * rows, :] + b1_ref[...]
        mask = plane_mask(x, rows, space, last, core)
        sig = jax.nn.sigmoid(y1)
        d_ref[x] = (sig * (1.0 + y1 * (1.0 - sig)) * mask).reshape(wide, ROWS, MID_L)
        act = (y1 * sig * mask).astype(BF)
        a_ref[x, :, :, :MID_L] = act.reshape(wide, ROWS, MID_L)
        edge = edges(act.astype(F32), 0, 128)
        a_ref[x, :, :, MID_L:] = edge.astype(BF).reshape(wide, ROWS, 128)
    narrow = wide - 2
    total = None
    for tap in range(9):
        a, b = divmod(tap, 3)
        part = dot(a_ref[a : a + 2, b : b + narrow].reshape(-1, 384), f2_ref[tap], NT)
        total = part if total is None else total + part
    y2 = total + b2_ref[...]
    sig = jax.nn.sigmoid(y2)
    shape = o_ref.shape
    o_ref[...] = (y2 * sig).astype(BF).reshape(shape)
    cot = c_ref[...].reshape(-1, MID_L).astype(F32)
    g_ref[...] = (cot * (sig * (1.0 + y2 * (1.0 - sig)))).astype(BF).reshape(shape)


def flipped(grads):
    turned = grads.astype(F32).T
    sums = jnp.sum(turned, axis=1, keepdims=True)
    bias = sums[0:64] + sums[64:128] + sums[128:192] + sums[192:256]
    return turned.astype(BF), bias


def tap_sum(product, step):
    frame = product.shape[1]
    total = product[64:128]
    for j in (0, 2, 3):
        total = total + pltpu.roll(product[j * 64 : (j + 1) * 64], (frame - (j - 1) * step) % frame, 1)
    return total


def second_weights_body(a_ref, g_ref, p_ref):
    turned, bias = flipped(g_ref[...].reshape(-1, MID_L))
    narrow = g_ref.shape[1]
    lane = lax.broadcasted_iota(jnp.int32, (64, 384), 1)
    held = None
    for tap in range(9):
        a, b = divmod(tap, 3)
        found = tap_sum(dot(turned, a_ref[a : a + 2, b : b + narrow].reshape(-1, 384), NN), C_MID)
        if tap == 8:
            p_ref[:, 1536:1792] = jnp.where(lane < TAP2, found, bias)[:, :256]
        elif tap % 2 == 0:
            held = found
        else:
            at = (tap - 1) * TAP2
            p_ref[:, at : at + 384] = jnp.where(lane < TAP2, held, pltpu.roll(found, TAP2, 1))


def backward_body(g_ref, l_ref, r_ref, y_ref, r2_ref, d_ref, e_ref, p2_ref, k_ref, s_ref, t_ref, wide_g, acc, pack):
    core = lax.axis_index("ysp")
    planes = [ref[i] for ref in (l_ref, g_ref, r_ref) for i in range(2)]
    spread(planes, y_ref, core, wide_g, MID_L)
    narrow = g_ref.shape[1]
    wide = narrow + 2
    total = None
    for tap in range(9):
        a, b = divmod(tap, 3)
        part = dot(wide_g[2 - a : 6 - a, 2 - b : 2 - b + wide].reshape(-1, 384), r2_ref[tap], NN)
        total = part if total is None else total + part
    acc[...] = total
    rows = wide * ROWS
    for x in range(4):
        slope = d_ref[x].reshape(rows, MID_L)
        g1 = (acc[x * rows : (x + 1) * rows, :] * slope).astype(BF)
        t_ref[x, :, :, :MID_L] = g1.reshape(wide, ROWS, MID_L)
        edge = edges(g1.astype(F32), 0, 128)
        t_ref[x, :, :, MID_L:] = edge.astype(BF).reshape(wide, ROWS, 128)
    turned, bias = flipped(t_ref[1:3, 1 : 1 + narrow, :, :MID_L].reshape(-1, MID_L))
    lane = lax.broadcasted_iota(jnp.int32, (64, 384), 1)
    none = jnp.zeros((64, 128), F32)
    held = None
    pack[:, :PACK2] = p2_ref[...]
    for tap in range(9):
        a, b = divmod(tap, 3)
        cells = e_ref[1 + a : 3 + a, 1 + b : 1 + b + narrow].reshape(-1, 256)
        found = tap_sum(dot(turned, cells, NN), C_IN)
        if tap == 8:
            pack[:, PACK2 + 768 : PACK2 + 896] = jnp.where(lane < TAP1, jnp.concatenate([found, none], axis=1), bias)[:, :128]
            continue
        found = jnp.concatenate([found, none], axis=1)
        slot = tap % 4
        if slot == 0:
            held = found
        else:
            held = jnp.where(lane < slot * TAP1, held, pltpu.roll(found, slot * TAP1, 1))
        if slot == 3:
            at = PACK2 + (tap - 3) * TAP1
            pack[:, at : at + 384] = held
    k_ref[...] = pack[pl.ds(core * 32, 32), :]
    s_ref[...] = pack[pl.ds((1 - core) * 32, 32), :].astype(BF)


def input_grad_body(t_ref, r1_ref, o_ref):
    narrow = o_ref.shape[1]
    total = None
    for tap in range(9):
        a, b = divmod(tap, 3)
        part = dot(t_ref[2 - a : 4 - a, 2 - b : 2 - b + narrow].reshape(-1, 384), r1_ref[tap], NN)
        total = part if total is None else total + part
    o_ref[...] = total.astype(BF).reshape(o_ref.shape)


def finish_body(m_ref, h_ref, w1_ref, b1_ref, w2_ref, b2_ref, pack):
    core = lax.axis_index("ysp")
    pack[pl.ds(core * 32, 32), :] = m_ref[...].astype(F32)
    pack[pl.ds((1 - core) * 32, 32), :] = h_ref[...].astype(F32)
    w2_ref[...] = pack[:, :W2_L]
    w1_ref[...] = pack[:, PACK2 : PACK2 + W1_L]
    row = lax.broadcasted_iota(jnp.int32, (64, 64), 0)
    col = lax.broadcasted_iota(jnp.int32, (64, 64), 1)
    for ref, at in ((b2_ref, W2_L), (b1_ref, PACK2 + W1_L)):
        spot = jnp.broadcast_to(pack[:, at : at + 1], (64, 64))
        ref[...] = jnp.sum(jnp.where(row == col, spot, 0.0), axis=0, keepdims=True)


def beside(cells, axis):
    last = lax.axis_size(axis) - 1
    return (
        lax.ppermute(cells, axis, [(i, i + 1) for i in range(last)]),
        lax.ppermute(cells, axis, [(i + 1, i) for i in range(last)]),
    )


def swap(cells, axis, bit):
    return lax.ppermute(cells, axis, [(i, i ^ bit) for i in range(lax.axis_size(axis))])


def other_core(left, own, right):
    wide = own.shape[1]
    start = (1 - lax.axis_index("ysp")) * (wide - 2)
    cols = [lax.dynamic_slice_in_dim(part, start, 2, axis=1) for part in (left, own, right)]
    return swap(jnp.concatenate(cols, axis=0), "ysp", 1)


def on_device(inputs, w_first, b_first, w_second, b_second, cotangent):
    nx, ny = inputs.shape[1], inputs.shape[2]
    cells = inputs.reshape(nx, ny, ROWS, IN_L)
    left, right = beside(cells, "space")
    f1, f2, r2, r1 = call(
        banded_body,
        [((9, 256, 256), BF), ((9, 256, 384), BF), ((9, 384, 256), BF), ((9, 384, 128), BF)],
        [pltpu.VMEM((64, 1152), F32), pltpu.VMEM((64, 2048), F32)],
    )(w_first.T, w_second.T)
    bias1 = jnp.tile(b_first, GROUP).reshape(1, MID_L)
    bias2 = jnp.tile(b_second, GROUP).reshape(1, MID_L)
    cot = cotangent.reshape(nx, ny, ROWS, MID_L)
    across = other_core(left, cells, right)
    wide_in, act, slope, out, g2 = call(
        forward_body,
        [
            ((nx + 4, ny + 4, ROWS, 256), BF),
            ((nx + 2, ny + 2, ROWS, 384), BF),
            ((nx + 2, ny + 2, ROWS, MID_L), F32),
            ((nx, ny, ROWS, MID_L), BF),
            ((nx, ny, ROWS, MID_L), BF),
        ],
        [pltpu.VMEM(((nx + 2) * (ny + 2) * ROWS, MID_L), F32)],
    )(cells, left, right, across, f1, f2, bias1, bias2, cot)
    g_left, g_right = beside(g2, "space")
    (pack2,) = call(second_weights_body, [((64, PACK2), F32)])(act, g2)
    g_across = other_core(g_left, g2, g_right)
    keep, send, turned = call(
        backward_body,
        [((32, PACK2 + PACK1), F32), ((32, PACK2 + PACK1), BF), ((nx + 2, ny + 2, ROWS, 384), BF)],
        [
            pltpu.VMEM((nx + 4, ny + 4, ROWS, 384), BF),
            pltpu.VMEM(((nx + 2) * (ny + 2) * ROWS, MID_L), F32),
            pltpu.VMEM((64, PACK2 + PACK1), F32),
        ],
    )(g2, g_left, g_right, g_across, r2, slope, wide_in, pack2)
    got = swap(send, "ysp", 1)
    total = lax.optimization_barrier((keep + got.astype(F32)).astype(BF))
    (d_in,) = call(input_grad_body, [((nx, ny, ROWS, IN_L), BF)])(turned, r1)
    for axis in ("dp", "space"):
        bit = 1
        while bit < lax.axis_size(axis):
            total = lax.optimization_barrier(total + swap(total, axis, bit))
            bit *= 2
    other = swap(total, "ysp", 1)
    gw1, gb1, gw2, gb2 = call(
        finish_body,
        [((64, W1_L), F32), ((1, 64), F32), ((64, W2_L), F32), ((1, 64), F32)],
        [pltpu.VMEM((64, PACK2 + PACK1), F32)],
    )(total, other)
    output = out.reshape(1, nx, ny, DEPTH * C_MID)
    input_grad = d_in.reshape(1, nx, ny, DEPTH * C_IN)
    return (output, input_grad, gw1.T, gb1.reshape(64), gw2.T, gb2.reshape(64))


def solution(mesh):
    placed = P(("groups", "dp"), "space", "ysp", None)
    return jax.shard_map(
        on_device,
        mesh=mesh,
        in_specs=(placed, P(), P(), P(), P(), placed),
        out_specs=(placed, placed, P("groups", None), P("groups"), P("groups", None), P("groups")),
        check_vma=False,
    )
```

```python
import jax
import jax.numpy as jnp
from jax import lax
from jax.experimental import pallas as pl
from jax.experimental.pallas import tpu as pltpu
from jax.sharding import PartitionSpec as P

C_IN = 32
C_MID = 64
DEPTH = 64
BF = jnp.bfloat16
F32 = jnp.float32
GROUP = 4
ROWS = DEPTH // GROUP
IN_L = GROUP * C_IN
MID_L = GROUP * C_MID
TAP1 = 3 * C_IN
TAP2 = 3 * C_MID
W1_L = 9 * TAP1
W2_L = 9 * TAP2
PACK2 = 1792
PACK1 = 896
NT = (((1,), (1,)), ((), ()))
NN = (((1,), (0,)), ((), ()))


def call(body, flops, outs, scratch=(), vmem=16 << 20, **specs):
    return pl.pallas_call(
        body,
        out_shape=[jax.ShapeDtypeStruct(shape, kind) for shape, kind in outs],
        scratch_shapes=list(scratch),
        compiler_params=pltpu.CompilerParams(vmem_limit_bytes=vmem),
        cost_estimate=pl.CostEstimate(flops=flops, bytes_accessed=flops // 256, transcendentals=0),
        **specs,
    )


def dot(a, b, dims):
    return lax.dot_general(a, b, dims, preferred_element_type=F32)


def window(ref, start, width):
    frame = 256 if width <= 128 else 384
    at = start // 128 * 128
    stop = min(at + frame, ref.shape[1])
    value = ref[:, at:stop]
    if stop < at + frame:
        value = jnp.concatenate([value, jnp.zeros((64, at + frame - stop), F32)], axis=1)
    if start != at:
        value = pltpu.roll(value, frame - (start - at), 1)
    lane = lax.broadcasted_iota(jnp.int32, value.shape, 1)
    return jnp.where(lane < width, value, 0.0)


def banded_body(w1_ref, w2_ref, b1_ref, b2_ref, f1_ref, f2_ref, r2_ref, r1_ref, bias_ref, pad1, pad2, lines, sems):
    copies = [
        pltpu.make_async_copy(w1_ref, pad1, sems.at[0]),
        pltpu.make_async_copy(w2_ref, pad2, sems.at[1]),
        pltpu.make_async_copy(b1_ref, lines.at[pl.ds(0, 1)], sems.at[2]),
        pltpu.make_async_copy(b2_ref, lines.at[pl.ds(1, 1)], sems.at[3]),
    ]
    for copy in copies:
        copy.start()
    for copy in copies:
        copy.wait()
    bias_ref[...] = jnp.concatenate([lines[...]] * GROUP, axis=1)
    for tap in range(9):
        one = window(pad1, tap * TAP1, TAP1)
        two = window(pad2, tap * TAP2, TAP2)
        for m in range(-1, 5):
            at = (m % 6) * C_MID
            s1 = pltpu.roll(one, ((m - 1) * C_IN) % 256, 1) if m != 1 else one
            s2 = pltpu.roll(two, ((m - 1) * C_MID) % 384, 1) if m != 1 else two
            s1 = s1.astype(BF)
            s2 = s2.astype(BF)
            if 0 <= m < 4:
                f1_ref[tap, m * C_MID : (m + 1) * C_MID, :] = s1
                f2_ref[tap, m * C_MID : (m + 1) * C_MID, :] = s2
            r1_ref[tap, at : at + C_MID, :] = s1[:, :IN_L]
            r2_ref[tap, at : at + C_MID, :] = s2[:, :MID_L]


def edges(value, low, high):
    count = value.shape[0]
    row = lax.broadcasted_iota(jnp.int32, (count, 128), 0) % ROWS
    lane = lax.broadcasted_iota(jnp.int32, (count, 128), 1)
    after = pltpu.roll(value[:, low : low + 128], count - 1, 0)
    before = pltpu.roll(value[:, high : high + 128], 1, 0)
    after = jnp.where(row == ROWS - 1, 0.0, after)
    before = jnp.where(row == 0, 0.0, before)
    return jnp.where(lane < 64, after, before)


def spread(parts, core, to_ref, lanes):
    for x, (middle, side) in enumerate(parts):
        side = side.astype(F32)
        low = jnp.where(core == 1, side, 0.0)
        high = jnp.where(core == 0, side, 0.0)
        cells = jnp.concatenate([low, middle.astype(F32), high], axis=0)
        rows = cells.reshape(-1, lanes)
        shape = cells.shape[:2]
        to_ref[x, :, :, :lanes] = cells.astype(BF)
        edge = edges(rows, 0, lanes - 128)
        to_ref[x, :, :, lanes:] = edge.astype(BF).reshape(*shape, 128)


def gathered(own, even, odd, beside, core, space, width):
    count, depth = own.shape[0], even.shape[0]
    end = own.shape[1]
    head, tail = pl.ds(0, width), pl.ds(end - width, width)

    def near(i):
        return jnp.where(core == 0, beside[i, head], beside[i, tail])

    flip = space % 2 == 1
    one = [(even[i], near(i)) for i in range(depth)]
    two = [(odd[i], near(depth + count + i)) for i in range(depth)]
    left = [(jnp.where(flip, p[0], q[0]), jnp.where(flip, p[1], q[1])) for p, q in zip(one, two)]
    right = [(jnp.where(flip, q[0], p[0]), jnp.where(flip, q[1], p[1])) for p, q in zip(one, two)]
    return left + [(own[i], near(depth + i)) for i in range(count)] + right


def plane_mask(x, rows, space, last, core):
    row = lax.broadcasted_iota(jnp.int32, (rows, 1), 0)
    inside = jnp.float32(1.0)
    if x == 0:
        inside = jnp.where(space > 0, 1.0, 0.0)
    if x == 3:
        inside = jnp.where(space < last, 1.0, 0.0)
    low = jnp.where(core == 1, 1.0, 0.0)
    high = jnp.where(core == 0, 1.0, 0.0)
    mask = jnp.where(row < ROWS, low, jnp.where(row >= rows - ROWS, high, 1.0))
    return mask * inside


def forward_body(x_ref, ev_ref, od_ref, by_ref, f1_ref, f2_ref, b_ref, c_ref, e_ref, a_ref, d_ref, o_ref, g_ref, acc):
    core = lax.axis_index("ysp")
    space = lax.axis_index("space")
    last = lax.axis_size("space") - 1
    spread(gathered(x_ref, ev_ref, od_ref, by_ref, core, space, 2), core, e_ref, IN_L)
    wide = x_ref.shape[1] + 2
    narrow = wide - 2
    total = None
    for tap in range(9):
        a, b = divmod(tap, 3)
        part = dot(e_ref[a : a + 4, b : b + wide].reshape(-1, 256), f1_ref[tap], NT)
        total = part if total is None else total + part
    acc[...] = total
    rows = wide * ROWS
    bias1, bias2 = b_ref[0:1], b_ref[1:2]
    for x in range(4):
        y1 = acc[x * rows : (x + 1) * rows, :] + bias1
        mask = plane_mask(x, rows, space, last, core)
        sig = jax.nn.sigmoid(y1)
        d_ref[x] = (sig * (1.0 + y1 * (1.0 - sig)) * mask).reshape(wide, ROWS, MID_L)
        act = (y1 * sig * mask).astype(BF)
        a_ref[x, :, :, :MID_L] = act.reshape(wide, ROWS, MID_L)
        edge = edges(act.astype(F32), 0, 128)
        a_ref[x, :, :, MID_L:] = edge.astype(BF).reshape(wide, ROWS, 128)
    total = None
    for tap in range(9):
        a, b = divmod(tap, 3)
        part = dot(a_ref[a : a + 2, b : b + narrow].reshape(-1, 384), f2_ref[tap], NT)
        total = part if total is None else total + part
    y2 = total + bias2
    sig = jax.nn.sigmoid(y2)
    shape = o_ref.shape
    o_ref[...] = (y2 * sig).astype(BF).reshape(shape)
    cot = c_ref[...].reshape(-1, MID_L).astype(F32)
    g_ref[...] = (cot * (sig * (1.0 + y2 * (1.0 - sig)))).astype(BF).reshape(shape)


def flipped(grads):
    turned = grads.astype(F32).T
    sums = jnp.sum(turned, axis=1, keepdims=True)
    bias = sums[0:64] + sums[64:128] + sums[128:192] + sums[192:256]
    return turned.astype(BF), bias


def tap_sum(product, step):
    frame = product.shape[1]
    total = product[64:128]
    for j in (0, 2, 3):
        total = total + pltpu.roll(product[j * 64 : (j + 1) * 64], (frame - (j - 1) * step) % frame, 1)
    return total


def second_weights_body(a_ref, g_ref, k_ref, s_ref, p_ref):
    turned, bias = flipped(g_ref[...].reshape(-1, MID_L))
    narrow = g_ref.shape[1]
    lane = lax.broadcasted_iota(jnp.int32, (64, 384), 1)
    held = None
    for tap in range(9):
        a, b = divmod(tap, 3)
        found = tap_sum(dot(turned, a_ref[a : a + 2, b : b + narrow].reshape(-1, 384), NN), C_MID)
        if tap == 8:
            p_ref[:, 1536:1792] = jnp.where(lane < TAP2, found, bias)[:, :256]
        elif tap % 2 == 0:
            held = found
        else:
            at = (tap - 1) * TAP2
            p_ref[:, at : at + 384] = jnp.where(lane < TAP2, held, pltpu.roll(found, TAP2, 1))
    halves(p_ref, k_ref, s_ref)


def halves(pack, keep_ref, send_ref):
    core = lax.axis_index("ysp")
    keep_ref[...] = pack[pl.ds(core * 32, 32), :]
    send_ref[...] = pack[pl.ds((1 - core) * 32, 32), :].astype(BF)


def adjoint(wide_ref, taps_ref, tall, wide):
    total = None
    for tap in range(9):
        a, b = divmod(tap, 3)
        part = dot(wide_ref[2 - a : 2 - a + tall, 2 - b : 2 - b + wide].reshape(-1, 384), taps_ref[tap], NN)
        total = part if total is None else total + part
    return total


def backward_body(g_ref, ev_ref, od_ref, by_ref, r2_ref, d_ref, e_ref, k_ref, s_ref, t_ref, wide_g, acc, pack):
    core = lax.axis_index("ysp")
    space = lax.axis_index("space")
    spread(gathered(g_ref, ev_ref, od_ref, by_ref, core, space, 2), core, wide_g, MID_L)
    narrow = g_ref.shape[1]
    wide = narrow + 2
    rows = wide * ROWS
    acc[...] = adjoint(wide_g, r2_ref, 4, wide)
    for x in range(4):
        slope = d_ref[x].reshape(rows, MID_L)
        g1 = (acc[x * rows : (x + 1) * rows, :] * slope).astype(BF)
        t_ref[x, :, :, :MID_L] = g1.reshape(wide, ROWS, MID_L)
        edge = edges(g1.astype(F32), 0, 128)
        t_ref[x, :, :, MID_L:] = edge.astype(BF).reshape(wide, ROWS, 128)
    g1 = t_ref[1:3, 1 : 1 + narrow, :, :MID_L].reshape(-1, MID_L)
    turned, bias = flipped(g1)
    lane = lax.broadcasted_iota(jnp.int32, (64, 384), 1)
    none = jnp.zeros((64, 128), F32)
    held = None
    for tap in range(9):
        a, b = divmod(tap, 3)
        cells = e_ref[1 + a : 3 + a, 1 + b : 1 + b + narrow].reshape(-1, 256)
        found = tap_sum(dot(turned, cells, NN), C_IN)
        if tap == 8:
            pack[:, 768:896] = jnp.where(lane < TAP1, jnp.concatenate([found, none], axis=1), bias)[:, :128]
            continue
        found = jnp.concatenate([found, none], axis=1)
        slot = tap % 4
        if slot == 0:
            held = found
        else:
            held = jnp.where(lane < slot * TAP1, held, pltpu.roll(found, slot * TAP1, 1))
        if slot == 3:
            at = (tap - 3) * TAP1
            pack[:, at : at + 384] = held
    halves(pack, k_ref, s_ref)


def input_grad_body(t_ref, r1_ref, o_ref):
    o_ref[...] = adjoint(t_ref, r1_ref, *o_ref.shape[:2]).astype(BF).reshape(o_ref.shape)


def finish_body(m_ref, h_ref, w2_ref, b2_ref, w1_ref, b1_ref, pack):
    core = lax.axis_index("ysp")
    pack[pl.ds(core * 32, 32), :] = m_ref[...].astype(F32)
    pack[pl.ds((1 - core) * 32, 32), :] = h_ref[...].astype(F32)
    row = lax.broadcasted_iota(jnp.int32, (64, 64), 0)
    col = lax.broadcasted_iota(jnp.int32, (64, 64), 1)
    for at, w_ref, b_ref in ((0, w2_ref, b2_ref), (PACK2, w1_ref, b1_ref)):
        width = w_ref.shape[1]
        w_ref[...] = pack[:, at : at + width]
        spot = jnp.broadcast_to(pack[:, at + width : at + width + 1], (64, 64))
        b_ref[...] = jnp.sum(jnp.where(row == col, spot, 0.0), axis=0, keepdims=True)


def swap(cells, axis, bit):
    return lax.ppermute(cells, axis, [(i, i ^ bit) for i in range(lax.axis_size(axis))])


def halo(own, even, odd):
    count = lax.axis_size("space")
    pairs = [(i, i + 1) for i in range(1, count - 1, 2)]
    odd = lax.ppermute(odd, "space", pairs + [(j, i) for i, j in pairs])
    pairs = [(i, i + 1) for i in range(0, count - 1, 2)]
    even = lax.ppermute(even, "space", pairs + [(j, i) for i, j in pairs])
    return even, odd


def other_core(own, even, odd):
    return swap(jnp.concatenate([even, own, odd], axis=0), "ysp", 1)


hold = lax.optimization_barrier


def first_half(keep, send):
    return hold((keep + swap(send, "ysp", 1).astype(F32)).astype(BF))


def masks(axis):
    return [(axis, 2 * m - 1) for m in (1, 2, 4, 8, 16, 32, 64) if m < lax.axis_size(axis)]


def stage(total, axis, mask):
    return hold(total + swap(total, axis, mask))


def on_device(inputs, w_first, b_first, w_second, b_second, cotangent):
    nx, ny = inputs.shape[1], inputs.shape[2]
    own = inputs.reshape(nx, ny, ROWS, IN_L)
    even, odd = halo(own, own, own)
    hbm = pl.BlockSpec(memory_space=pltpu.HBM)
    banded = call(
        banded_body,
        2000000000,
        [
            ((9, 256, 256), BF),
            ((9, 256, 384), BF),
            ((9, 384, 256), BF),
            ((9, 384, 128), BF),
            ((2, MID_L), F32),
        ],
        [
            pltpu.VMEM((64, W1_L), F32),
            pltpu.VMEM((64, W2_L), F32),
            pltpu.VMEM((2, C_MID), F32),
            pltpu.SemaphoreType.DMA((4,)),
        ],
        vmem=16 << 20,
        in_specs=[hbm] * 4,
    )(*[pltpu.with_memory_space_constraint(v, pltpu.HBM) for v in (w_first.T, w_second.T, b_first.reshape(1, C_MID), b_second.reshape(1, C_MID))])
    cot = cotangent.reshape(nx, ny, ROWS, MID_L)
    even, odd, cot, f1, f2, r2, r1, bias = hold((even, odd, cot, *banded))
    wide_in, act, slope, out, g2 = call(
        forward_body,
        4800000000,
        [
            ((nx + 4, ny + 4, ROWS, 256), BF),
            ((nx + 2, ny + 2, ROWS, 384), BF),
            ((nx + 2, ny + 2, ROWS, MID_L), F32),
            ((nx, ny, ROWS, MID_L), BF),
            ((nx, ny, ROWS, MID_L), BF),
        ],
        [pltpu.VMEM(((nx + 2) * (ny + 2) * ROWS, MID_L), F32)],
    )(own, even, odd, other_core(own, even, odd), f1, f2, bias, cot)
    even, odd = halo(g2, g2, g2)
    keep2, send2 = call(
        second_weights_body, 1800000000, [((32, PACK2), F32), ((32, PACK2), BF)], [pltpu.VMEM((64, PACK2), F32)]
    )(act, g2)
    *early, final = masks("dp") + masks("space")
    even, odd, keep2, send2 = hold((even, odd, keep2, send2))
    sum2 = first_half(keep2, send2)
    got2 = swap(sum2, *early[0])
    keep1, send1, wide_g = call(
        backward_body,
        5600000000,
        [((32, PACK1), F32), ((32, PACK1), BF), ((nx + 2, ny + 2, ROWS, 384), BF)],
        [
            pltpu.VMEM((nx + 4, ny + 4, ROWS, 384), BF),
            pltpu.VMEM(((nx + 2) * (ny + 2) * ROWS, MID_L), F32),
            pltpu.VMEM((64, PACK1), F32),
        ],
    )(g2, even, odd, other_core(g2, even, odd), r2, slope, wide_in)
    got2, keep1, send1, wide_g = hold((got2, keep1, send1, wide_g))
    sum2 = hold(sum2 + got2)
    for axis, mask in early[1:]:
        sum2 = stage(sum2, axis, mask)
    sum1 = first_half(keep1, send1)
    (d_in,) = call(input_grad_body, 1200000000, [((nx, ny, ROWS, IN_L), BF)])(wide_g, r1)
    output = out.reshape(1, nx, ny, DEPTH * C_MID)
    input_grad = d_in.reshape(1, nx, ny, DEPTH * C_IN)
    sum2 = stage(sum2, *final)
    for at, (axis, mask) in enumerate([*early, final]):
        got1 = swap(sum1, axis, mask)
        if at == 0:
            got1, output, input_grad = hold((got1, output, input_grad))
        sum1 = hold(sum1 + got1)
    total = jnp.concatenate([sum2, sum1], axis=1)
    gw2, gb2, gw1, gb1 = call(
        finish_body,
        1200000000,
        [((64, W2_L), F32), ((1, 64), F32), ((64, W1_L), F32), ((1, 64), F32)],
        [pltpu.VMEM((64, PACK2 + PACK1), F32)],
    )(total, swap(total, "ysp", 1))
    return (output, input_grad, gw1.T, gb1.reshape(64), gw2.T, gb2.reshape(64))


def solution(mesh):
    placed = P(("groups", "dp"), "space", "ysp", None)
    return jax.shard_map(
        on_device,
        mesh=mesh,
        in_specs=(placed, P(), P(), P(), P(), placed),
        out_specs=(placed, placed, P("groups", None), P("groups"), P("groups", None), P("groups")),
        check_vma=False,
    )
```

```python
import jax
import jax.numpy as jnp
from jax import lax
from jax.experimental import pallas as pl
from jax.experimental.pallas import tpu as pltpu
from jax.sharding import PartitionSpec as P

C_IN = 32
C_MID = 64
DEPTH = 64
BF = jnp.bfloat16
F32 = jnp.float32
GROUP = 4
ROWS = DEPTH // GROUP
IN_L = GROUP * C_IN
MID_L = GROUP * C_MID
TAP1 = 3 * C_IN
TAP2 = 3 * C_MID
W1_L = 9 * TAP1
W2_L = 9 * TAP2
PACK2 = 1792
PACK1 = 896
NT = (((1,), (1,)), ((), ()))
NN = (((1,), (0,)), ((), ()))


def call(body, flops, outs, scratch=(), vmem=16 << 20, **specs):
    return pl.pallas_call(
        body,
        out_shape=[jax.ShapeDtypeStruct(shape, kind) for shape, kind in outs],
        scratch_shapes=list(scratch),
        compiler_params=pltpu.CompilerParams(vmem_limit_bytes=vmem),
        cost_estimate=pl.CostEstimate(flops=flops, bytes_accessed=flops // 256, transcendentals=0),
        **specs,
    )


def dot(a, b, dims):
    return lax.dot_general(a, b, dims, preferred_element_type=F32)


def window(ref, start, width):
    frame = 256 if width <= 128 else 384
    at = start // 128 * 128
    stop = min(at + frame, ref.shape[1])
    value = ref[:, at:stop]
    if stop < at + frame:
        value = jnp.concatenate([value, jnp.zeros((64, at + frame - stop), F32)], axis=1)
    if start != at:
        value = pltpu.roll(value, frame - (start - at), 1)
    lane = lax.broadcasted_iota(jnp.int32, value.shape, 1)
    return jnp.where(lane < width, value, 0.0)


def banded_body(w1_ref, w2_ref, b1_ref, b2_ref, f1_ref, f2_ref, r2_ref, r1_ref, bias_ref, pad1, pad2, lines, sems):
    copies = [
        pltpu.make_async_copy(w1_ref, pad1, sems.at[0]),
        pltpu.make_async_copy(w2_ref, pad2, sems.at[1]),
        pltpu.make_async_copy(b1_ref, lines.at[pl.ds(0, 1)], sems.at[2]),
        pltpu.make_async_copy(b2_ref, lines.at[pl.ds(1, 1)], sems.at[3]),
    ]
    for copy in copies:
        copy.start()
    for copy in copies:
        copy.wait()
    bias_ref[...] = jnp.concatenate([lines[...]] * GROUP, axis=1)
    for tap in range(9):
        one = window(pad1, tap * TAP1, TAP1)
        two = window(pad2, tap * TAP2, TAP2)
        for m in range(-1, 5):
            at = (m % 6) * C_MID
            s1 = pltpu.roll(one, ((m - 1) * C_IN) % 256, 1) if m != 1 else one
            s2 = pltpu.roll(two, ((m - 1) * C_MID) % 384, 1) if m != 1 else two
            s1 = s1.astype(BF)
            s2 = s2.astype(BF)
            if 0 <= m < 4:
                f1_ref[m * C_MID : (m + 1) * C_MID, tap * 256 : (tap + 1) * 256] = s1
                f2_ref[m * C_MID : (m + 1) * C_MID, tap * 384 : (tap + 1) * 384] = s2
            r1_ref[tap, at : at + C_MID, :] = s1[:, :IN_L]
            r2_ref[tap, at : at + C_MID, :] = s2[:, :MID_L]


def edges(value, low, high):
    count = value.shape[0]
    row = lax.broadcasted_iota(jnp.int32, (count, 128), 0) % ROWS
    lane = lax.broadcasted_iota(jnp.int32, (count, 128), 1)
    after = pltpu.roll(value[:, low : low + 128], count - 1, 0)
    before = pltpu.roll(value[:, high : high + 128], 1, 0)
    after = jnp.where(row == ROWS - 1, 0.0, after)
    before = jnp.where(row == 0, 0.0, before)
    return jnp.where(lane < 64, after, before)


def spread(parts, core, to_ref, lanes):
    for x, (middle, side) in enumerate(parts):
        side = side.astype(F32)
        low = jnp.where(core == 1, side, 0.0)
        high = jnp.where(core == 0, side, 0.0)
        cells = jnp.concatenate([low, middle.astype(F32), high], axis=0)
        rows = cells.reshape(-1, lanes)
        shape = cells.shape[:2]
        to_ref[x, :, :, :lanes] = cells.astype(BF)
        edge = edges(rows, 0, lanes - 128)
        to_ref[x, :, :, lanes:] = edge.astype(BF).reshape(*shape, 128)


def gathered(own, side, even, odd, space):
    count, narrow = own.shape[:2]
    both = [(even[i], odd[i]) for i in range(even.shape[0])]
    flip = space % 2 == 1
    left = [jnp.where(flip, one, two) for one, two in both]
    right = [jnp.where(flip, two, one) for one, two in both]
    mid = [(own[i], side[i]) for i in range(count)]
    return [(p[:narrow], p[narrow:]) for p in left] + mid + [(p[:narrow], p[narrow:]) for p in right]


def taps(of):
    parts = [of(*divmod(tap, 3)) for tap in range(9)]
    return jnp.concatenate([part.reshape(-1, part.shape[-1]) for part in parts], axis=1)


def sigmoid(value):
    return 0.5 * jnp.tanh(0.5 * value) + 0.5


def plane_mask(x, rows, space, last, core):
    row = lax.broadcasted_iota(jnp.int32, (rows, 1), 0)
    inside = jnp.float32(1.0)
    if x == 0:
        inside = jnp.where(space > 0, 1.0, 0.0)
    if x == 3:
        inside = jnp.where(space < last, 1.0, 0.0)
    low = jnp.where(core == 1, 1.0, 0.0)
    high = jnp.where(core == 0, 1.0, 0.0)
    mask = jnp.where(row < ROWS, low, jnp.where(row >= rows - ROWS, high, 1.0))
    return mask * inside


def forward_body(x_ref, by_ref, ev_ref, od_ref, f1_ref, f2_ref, b_ref, c_ref, e_ref, a_ref, d_ref, o_ref, g_ref, n_ref, acc):
    core = lax.axis_index("ysp")
    space = lax.axis_index("space")
    last = lax.axis_size("space") - 1
    spread(gathered(x_ref, by_ref, ev_ref, od_ref, space), core, e_ref, IN_L)
    wide = x_ref.shape[1] + 2
    narrow = wide - 2
    acc[...] = dot(taps(lambda a, b: e_ref[a : a + 4, b : b + wide]), f1_ref[...], NT)
    rows = wide * ROWS
    bias1, bias2 = b_ref[0:1], b_ref[1:2]
    for x in range(4):
        y1 = acc[x * rows : (x + 1) * rows, :] + bias1
        mask = plane_mask(x, rows, space, last, core)
        sig = sigmoid(y1)
        d_ref[x] = y1.reshape(wide, ROWS, MID_L)
        act = (y1 * sig * mask).astype(BF)
        a_ref[x, :, :, :MID_L] = act.reshape(wide, ROWS, MID_L)
        edge = edges(act.astype(F32), 0, 128)
        a_ref[x, :, :, MID_L:] = edge.astype(BF).reshape(wide, ROWS, 128)
    y2 = dot(taps(lambda a, b: a_ref[a : a + 2, b : b + narrow]), f2_ref[...], NT) + bias2
    sig = sigmoid(y2)
    shape = o_ref.shape
    o_ref[...] = (y2 * sig).astype(BF).reshape(shape)
    cot = c_ref[...].reshape(-1, MID_L).astype(F32)
    g_ref[...] = (cot * (sig * (1.0 + y2 * (1.0 - sig)))).astype(BF).reshape(shape)
    n_ref[...] = g_ref[:, pl.ds((1 - core) * (narrow - 2), 2)]


def flipped(grads):
    turned = grads.astype(F32).T
    sums = jnp.sum(turned, axis=1, keepdims=True)
    bias = sums[0:64] + sums[64:128] + sums[128:192] + sums[192:256]
    return turned.astype(BF), bias


def tap_sum(product, step):
    frame = product.shape[1]
    total = product[64:128]
    for j in (0, 2, 3):
        total = total + pltpu.roll(product[j * 64 : (j + 1) * 64], (frame - (j - 1) * step) % frame, 1)
    return total


def second_weights_body(a_ref, g_ref, y_ref, k_ref, s_ref, d_ref, p_ref):
    turned, bias = flipped(g_ref[...].reshape(-1, MID_L))
    narrow = g_ref.shape[1]
    lane = lax.broadcasted_iota(jnp.int32, (64, 384), 1)
    held = None
    for tap in range(9):
        a, b = divmod(tap, 3)
        found = tap_sum(dot(turned, a_ref[a : a + 2, b : b + narrow].reshape(-1, 384), NN), C_MID)
        if tap == 8:
            p_ref[:, 1536:1792] = jnp.where(lane < TAP2, found, bias)[:, :256]
        elif tap % 2 == 0:
            held = found
        else:
            at = (tap - 1) * TAP2
            p_ref[:, at : at + 384] = jnp.where(lane < TAP2, held, pltpu.roll(found, TAP2, 1))
    k_ref[...], s_ref[...] = halves(p_ref, lax.axis_index("dp") % 2)
    core = lax.axis_index("ysp")
    space = lax.axis_index("space")
    last = lax.axis_size("space") - 1
    rows = y_ref.shape[1] * ROWS
    for x in range(4):
        y1 = y_ref[x].reshape(rows, MID_L)
        sig = sigmoid(y1)
        slope = sig * (1.0 + y1 * (1.0 - sig)) * plane_mask(x, rows, space, last, core)
        d_ref[x] = slope.reshape(y_ref.shape[1:])


def halves(pack, which):
    count = pack.shape[0] // 2
    return pack[pl.ds(which * count, count), :], pack[pl.ds((1 - which) * count, count), :].astype(BF)


def adjoint(wide_ref, taps_ref, tall, wide):
    cells = taps(lambda a, b: wide_ref[2 - a : 2 - a + tall, 2 - b : 2 - b + wide])
    return dot(cells, taps_ref[...].reshape(9 * 384, -1), NN)


def backward_body(g_ref, by_ref, ev_ref, od_ref, r2_ref, d_ref, e_ref, k2_ref, h2_ref, k_ref, s_ref, t_ref, wide_g, acc, pack, pack2):
    core = lax.axis_index("ysp")
    space = lax.axis_index("space")
    spread(gathered(g_ref, by_ref, ev_ref, od_ref, space), core, wide_g, MID_L)
    narrow = g_ref.shape[1]
    wide = narrow + 2
    rows = wide * ROWS
    acc[...] = adjoint(wide_g, r2_ref, 4, wide)
    for x in range(4):
        slope = d_ref[x].reshape(rows, MID_L)
        g1 = (acc[x * rows : (x + 1) * rows, :] * slope).astype(BF)
        t_ref[x] = g1.reshape(wide, ROWS, MID_L)
    g1 = t_ref[1:3, 1 : 1 + narrow].reshape(-1, MID_L)
    turned, bias = flipped(g1)
    lane = lax.broadcasted_iota(jnp.int32, (64, 384), 1)
    none = jnp.zeros((64, 128), F32)
    held = None
    for tap in range(9):
        a, b = divmod(tap, 3)
        cells = e_ref[1 + a : 3 + a, 1 + b : 1 + b + narrow].reshape(-1, 256)
        found = tap_sum(dot(turned, cells, NN), C_IN)
        if tap == 8:
            pack[:, 768:896] = jnp.where(lane < TAP1, jnp.concatenate([found, none], axis=1), bias)[:, :128]
            continue
        found = jnp.concatenate([found, none], axis=1)
        slot = tap % 4
        if slot == 0:
            held = found
        else:
            held = jnp.where(lane < slot * TAP1, held, pltpu.roll(found, slot * TAP1, 1))
        if slot == 3:
            at = (tap - 3) * TAP1
            pack[:, at : at + 384] = held
    k_ref[:32], s_ref[:32] = halves(pack, core)
    pack2[...] = k2_ref[...] + h2_ref[...].astype(F32)
    keep, send = halves(pack2, core)
    k_ref[32:48], k_ref[48:] = keep[:, :PACK1], keep[:, PACK1:]
    s_ref[32:48], s_ref[48:] = send[:, :PACK1], send[:, PACK1:]


def input_grad_body(t_ref, r1_ref, o_ref, wide_g):
    for x in range(t_ref.shape[0]):
        wide_g[x, :, :, :MID_L] = t_ref[x]
        edge = edges(t_ref[x].reshape(-1, MID_L).astype(F32), 0, 128)
        wide_g[x, :, :, MID_L:] = edge.astype(BF).reshape(-1, ROWS, 128)
    o_ref[...] = adjoint(wide_g, r1_ref, *o_ref.shape[:2]).astype(BF).reshape(o_ref.shape)


def finish_body(m_ref, h_ref, w2_ref, b2_ref, w1_ref, b1_ref, pack2, pack1):
    core = lax.axis_index("ysp")
    first = lax.axis_index("dp") % 2
    for ref, of in ((m_ref, core), (h_ref, 1 - core)):
        for at, half in ((0, first), (32, 1 - first)):
            rows = pl.ds(half * 32 + of * 16, 16)
            pack2[rows, :PACK1] = ref[at : at + 16].astype(F32)
            pack2[rows, PACK1:] = ref[at + 16 : at + 32].astype(F32)
        pack1[pl.ds(of * 32, 32), :] = ref[64:].astype(F32)
    row = lax.broadcasted_iota(jnp.int32, (64, 64), 0)
    col = lax.broadcasted_iota(jnp.int32, (64, 64), 1)
    for pack, w_ref, b_ref in ((pack2, w2_ref, b2_ref), (pack1, w1_ref, b1_ref)):
        width = w_ref.shape[1]
        w_ref[...] = pack[:, :width]
        spot = jnp.broadcast_to(pack[:, width : width + 1], (64, 64))
        b_ref[...] = jnp.sum(jnp.where(row == col, spot, 0.0), axis=0, keepdims=True)


def swap(cells, axis, bit):
    return lax.ppermute(cells, axis, [(i, i ^ bit) for i in range(lax.axis_size(axis))])


def halo(own, edge):
    side = swap(edge, "ysp", 1)
    cells = jnp.concatenate([own, side], axis=1)
    count = lax.axis_size("space")
    pairs = [(i, i + 1) for i in range(1, count - 1, 2)]
    odd = lax.ppermute(cells, "space", pairs + [(j, i) for i, j in pairs])
    pairs = [(i, i + 1) for i in range(0, count - 1, 2)]
    even = lax.ppermute(cells, "space", pairs + [(j, i) for i, j in pairs])
    return side, even, odd


hold = lax.optimization_barrier


def powers(axis, first):
    return [m for m in (1, 2, 4, 8, 16, 32, 64) if first <= m < lax.axis_size(axis)]


def stage(total, axis, mask):
    return hold(total + swap(total, axis, mask))


def on_device(inputs, w_first, b_first, w_second, b_second, cotangent):
    nx, ny = inputs.shape[1], inputs.shape[2]
    own = inputs.reshape(nx, ny, ROWS, IN_L)
    edge = lax.dynamic_slice_in_dim(own, (1 - lax.axis_index("ysp")) * (ny - 2), 2, axis=1)
    side, even, odd = halo(own, edge)
    hbm = pl.BlockSpec(memory_space=pltpu.HBM)
    banded = call(
        banded_body,
        2000000000,
        [
            ((256, 9 * 256), BF),
            ((256, 9 * 384), BF),
            ((9, 384, 256), BF),
            ((9, 384, 128), BF),
            ((2, MID_L), F32),
        ],
        [
            pltpu.VMEM((64, W1_L), F32),
            pltpu.VMEM((64, W2_L), F32),
            pltpu.VMEM((2, C_MID), F32),
            pltpu.SemaphoreType.DMA((4,)),
        ],
        vmem=16 << 20,
        in_specs=[hbm] * 4,
    )(*[pltpu.with_memory_space_constraint(v, pltpu.HBM) for v in (w_first.T, w_second.T, b_first.reshape(1, C_MID), b_second.reshape(1, C_MID))])
    cot = cotangent.reshape(nx, ny, ROWS, MID_L)
    even, odd, cot, f1, f2, r2, r1, bias = hold((even, odd, cot, *banded))
    wide_in, act, y1, out, g2, edge = call(
        forward_body,
        4800000000,
        [
            ((nx + 4, ny + 4, ROWS, 256), BF),
            ((nx + 2, ny + 2, ROWS, 384), BF),
            ((nx + 2, ny + 2, ROWS, MID_L), F32),
            ((nx, ny, ROWS, MID_L), BF),
            ((nx, ny, ROWS, MID_L), BF),
            ((nx, 2, ROWS, MID_L), BF),
        ],
        [pltpu.VMEM(((nx + 2) * (ny + 2) * ROWS, MID_L), F32)],
    )(own, side, even, odd, f1, f2, bias, cot)
    side, even, odd = halo(g2, edge)
    keep2, send2, slope = call(
        second_weights_body,
        1800000000,
        [((32, PACK2), F32), ((32, PACK2), BF), ((nx + 2, ny + 2, ROWS, MID_L), F32)],
        [pltpu.VMEM((64, PACK2), F32)],
    )(act, g2, y1)
    got2 = swap(send2, "dp", 1)
    even, odd, keep2, got2 = hold((even, odd, keep2, got2))
    keep, send, g1 = call(
        backward_body,
        5600000000,
        [((64, PACK1), F32), ((64, PACK1), BF), ((nx + 2, ny + 2, ROWS, MID_L), BF)],
        [
            pltpu.VMEM((nx + 4, ny + 4, ROWS, 384), BF),
            pltpu.VMEM(((nx + 2) * (ny + 2) * ROWS, MID_L), F32),
            pltpu.VMEM((64, PACK1), F32),
            pltpu.VMEM((32, PACK2), F32),
        ],
    )(g2, side, even, odd, r2, slope, wide_in, keep2, got2)
    total = hold((keep + swap(send, "ysp", 1).astype(F32)).astype(BF))
    sum1, sum2 = hold((total[:32], total[32:]))
    (d_in,) = call(
        input_grad_body,
        1200000000,
        [((nx, ny, ROWS, IN_L), BF)],
        [pltpu.VMEM((nx + 2, ny + 2, ROWS, 384), BF)],
    )(g1, r1)
    output = out.reshape(1, nx, ny, DEPTH * C_MID)
    input_grad = d_in.reshape(1, nx, ny, DEPTH * C_IN)
    along = [("space", 2 * m - 1) for m in powers("space", 1)]
    stages1 = [("dp", m) for m in powers("dp", 1)] + along
    stages2 = [("dp", m) for m in powers("dp", 2)] + along
    for at, (one, two) in enumerate(zip(stages1, [*stages2, None])):
        got1 = swap(sum1, *one)
        got2 = swap(sum2, *two) if two else swap(sum2, "dp", 1)
        if at == 1:
            got1, output = hold((got1, output))
        if at == 1:
            got1, input_grad = hold((got1, input_grad))
        sum1 = hold(sum1 + got1)
        if two:
            sum2 = hold(sum2 + got2)
    total = jnp.concatenate([sum2, got2, sum1], axis=0)
    gw2, gb2, gw1, gb1 = call(
        finish_body,
        1200000000,
        [((64, W2_L), F32), ((1, 64), F32), ((64, W1_L), F32), ((1, 64), F32)],
        [pltpu.VMEM((64, PACK2), F32), pltpu.VMEM((64, PACK1), F32)],
    )(total, swap(total, "ysp", 1))
    return (output, input_grad, gw1.T, gb1.reshape(64), gw2.T, gb2.reshape(64))


def solution(mesh):
    placed = P(("groups", "dp"), "space", "ysp", None)
    return jax.shard_map(
        on_device,
        mesh=mesh,
        in_specs=(placed, P(), P(), P(), P(), placed),
        out_specs=(placed, placed, P("groups", None), P("groups"), P("groups", None), P("groups")),
        check_vma=False,
    )
```

```python
import jax
import jax.numpy as jnp
from jax import lax
from jax.experimental import pallas as pl
from jax.experimental.pallas import tpu as pltpu
from jax.sharding import PartitionSpec as P

C_IN = 32
C_MID = 64
DEPTH = 64
BF = jnp.bfloat16
F32 = jnp.float32
hold = lax.optimization_barrier
GROUP = 4
ROWS = DEPTH // GROUP
IN_L = GROUP * C_IN
MID_L = GROUP * C_MID
TAP1 = 3 * C_IN
TAP2 = 3 * C_MID
W1_L = 9 * TAP1
W2_L = 9 * TAP2
PACK2 = 1792
PACK1 = 896
NT = (((1,), (1,)), ((), ()))
NN = (((1,), (0,)), ((), ()))


def call(body, flops, outs, scratch=(), vmem=16 << 20, **specs):
    return pl.pallas_call(
        body,
        out_shape=[jax.ShapeDtypeStruct(shape, kind) for shape, kind in outs],
        scratch_shapes=list(scratch),
        compiler_params=pltpu.CompilerParams(vmem_limit_bytes=vmem),
        cost_estimate=pl.CostEstimate(flops=flops, bytes_accessed=flops // 256, transcendentals=0),
        **specs,
    )


def dot(a, b, dims):
    return lax.dot_general(a, b, dims, preferred_element_type=F32)


def window(ref, start, width):
    frame = 256 if width <= 128 else 384
    at = start // 128 * 128
    stop = min(at + frame, ref.shape[1])
    value = ref[:, at:stop]
    if stop < at + frame:
        value = jnp.concatenate([value, jnp.zeros((64, at + frame - stop), F32)], axis=1)
    if start != at:
        value = pltpu.roll(value, frame - (start - at), 1)
    lane = lax.broadcasted_iota(jnp.int32, value.shape, 1)
    return jnp.where(lane < width, value, 0.0)


def banded_body(w1_ref, w2_ref, b1_ref, b2_ref, f1_ref, f2_ref, r2_ref, r1_ref, bias_ref, pad1, pad2, lines, sems):
    copies = [
        pltpu.make_async_copy(w1_ref, pad1, sems.at[0]),
        pltpu.make_async_copy(w2_ref, pad2, sems.at[1]),
        pltpu.make_async_copy(b1_ref, lines.at[pl.ds(0, 1)], sems.at[2]),
        pltpu.make_async_copy(b2_ref, lines.at[pl.ds(1, 1)], sems.at[3]),
    ]
    for copy in copies:
        copy.start()
    for copy in copies:
        copy.wait()
    bias_ref[...] = jnp.concatenate([lines[...]] * GROUP, axis=1)
    for tap in range(9):
        one = window(pad1, tap * TAP1, TAP1)
        two = window(pad2, tap * TAP2, TAP2)
        for m in range(-1, 5):
            at = (m % 6) * C_MID
            s1 = pltpu.roll(one, ((m - 1) * C_IN) % 256, 1) if m != 1 else one
            s2 = pltpu.roll(two, ((m - 1) * C_MID) % 384, 1) if m != 1 else two
            s1 = s1.astype(BF)
            s2 = s2.astype(BF)
            if 0 <= m < 4:
                f1_ref[m * C_MID : (m + 1) * C_MID, tap * 256 : (tap + 1) * 256] = s1
                f2_ref[m * C_MID : (m + 1) * C_MID, tap * 384 : (tap + 1) * 384] = s2
            r1_ref[tap, at : at + C_MID, :] = s1[:, :IN_L]
            r2_ref[tap, at : at + C_MID, :] = s2[:, :MID_L]


def edges(value, low, high):
    count = value.shape[0]
    row = lax.broadcasted_iota(jnp.int32, (count, 128), 0) % ROWS
    lane = lax.broadcasted_iota(jnp.int32, (count, 128), 1)
    after = pltpu.roll(value[:, low : low + 128], count - 1, 0)
    before = pltpu.roll(value[:, high : high + 128], 1, 0)
    after = jnp.where(row == ROWS - 1, 0.0, after)
    before = jnp.where(row == 0, 0.0, before)
    return jnp.where(lane < 64, after, before)


def spread(parts, core, to_ref, lanes):
    for x, (middle, side) in enumerate(parts):
        side = side.astype(F32)
        low = jnp.where(core == 1, side, 0.0)
        high = jnp.where(core == 0, side, 0.0)
        cells = jnp.concatenate([low, middle.astype(F32), high], axis=0)
        rows = cells.reshape(-1, lanes)
        shape = cells.shape[:2]
        to_ref[x, :, :, :lanes] = cells.astype(BF)
        edge = edges(rows, 0, lanes - 128)
        to_ref[x, :, :, lanes:] = edge.astype(BF).reshape(*shape, 128)


def gathered(own, side, even, odd, space):
    count, narrow = own.shape[:2]
    both = [(even[i], odd[i]) for i in range(even.shape[0])]
    flip = space % 2 == 1
    left = [jnp.where(flip, one, two) for one, two in both]
    right = [jnp.where(flip, two, one) for one, two in both]
    mid = [(own[i], side[i]) for i in range(count)]
    return [(p[:narrow], p[narrow:]) for p in left] + mid + [(p[:narrow], p[narrow:]) for p in right]


def taps(of):
    parts = [of(*divmod(tap, 3)) for tap in range(9)]
    return jnp.concatenate([part.reshape(-1, part.shape[-1]) for part in parts], axis=1)


def sigmoid(value):
    return 0.5 * jnp.tanh(0.5 * value) + 0.5


def plane_mask(x, rows, space, last, core):
    row = lax.broadcasted_iota(jnp.int32, (rows, 1), 0)
    inside = jnp.float32(1.0)
    if x == 0:
        inside = jnp.where(space > 0, 1.0, 0.0)
    if x == 3:
        inside = jnp.where(space < last, 1.0, 0.0)
    low = jnp.where(core == 1, 1.0, 0.0)
    high = jnp.where(core == 0, 1.0, 0.0)
    mask = jnp.where(row < ROWS, low, jnp.where(row >= rows - ROWS, high, 1.0))
    return mask * inside


def forward_body(x_ref, by_ref, ev_ref, od_ref, f1_ref, f2_ref, b_ref, c_ref, e_ref, a_ref, d_ref, o_ref, g_ref, n_ref, acc):
    core = lax.axis_index("ysp")
    space = lax.axis_index("space")
    last = lax.axis_size("space") - 1
    spread(gathered(x_ref, by_ref, ev_ref, od_ref, space), core, e_ref, IN_L)
    wide = x_ref.shape[1] + 2
    narrow = wide - 2
    acc[...] = dot(taps(lambda a, b: e_ref[a : a + 4, b : b + wide]), f1_ref[...], NT)
    rows = wide * ROWS
    bias1, bias2 = b_ref[0:1], b_ref[1:2]
    for x in range(4):
        y1 = acc[x * rows : (x + 1) * rows, :] + bias1
        mask = plane_mask(x, rows, space, last, core)
        sig = sigmoid(y1)
        d_ref[x] = y1.reshape(wide, ROWS, MID_L)
        act = (y1 * sig * mask).astype(BF)
        a_ref[x, :, :, :MID_L] = act.reshape(wide, ROWS, MID_L)
        edge = edges(act.astype(F32), 0, 128)
        a_ref[x, :, :, MID_L:] = edge.astype(BF).reshape(wide, ROWS, 128)
    y2 = dot(taps(lambda a, b: a_ref[a : a + 2, b : b + narrow]), f2_ref[...], NT) + bias2
    sig = sigmoid(y2)
    shape = o_ref.shape
    o_ref[...] = (y2 * sig).astype(BF).reshape(shape)
    cot = c_ref[...].reshape(-1, MID_L).astype(F32)
    g_ref[...] = (cot * (sig * (1.0 + y2 * (1.0 - sig)))).astype(BF).reshape(shape)
    n_ref[...] = g_ref[:, pl.ds((1 - core) * (narrow - 2), 2)]


def flipped(grads):
    turned = grads.astype(F32).T
    sums = jnp.sum(turned, axis=1, keepdims=True)
    bias = sums[0:64] + sums[64:128] + sums[128:192] + sums[192:256]
    return turned.astype(BF), bias


def tap_sum(product, step):
    frame = product.shape[1]
    total = product[64:128]
    for j in (0, 2, 3):
        total = total + pltpu.roll(product[j * 64 : (j + 1) * 64], (frame - (j - 1) * step) % frame, 1)
    return total


def second_weights_body(a_ref, g_ref, y_ref, k_ref, s_ref, d_ref, p_ref):
    turned, bias = flipped(g_ref[...].reshape(-1, MID_L))
    narrow = g_ref.shape[1]
    lane = lax.broadcasted_iota(jnp.int32, (64, 384), 1)
    held = None
    for tap in range(9):
        a, b = divmod(tap, 3)
        found = tap_sum(dot(turned, a_ref[a : a + 2, b : b + narrow].reshape(-1, 384), NN), C_MID)
        if tap == 8:
            p_ref[:, 1536:1792] = jnp.where(lane < TAP2, found, bias)[:, :256]
        elif tap % 2 == 0:
            held = found
        else:
            at = (tap - 1) * TAP2
            p_ref[:, at : at + 384] = jnp.where(lane < TAP2, held, pltpu.roll(found, TAP2, 1))
    k_ref[...], s_ref[...] = halves(p_ref, lax.axis_index("dp") % 2)
    core = lax.axis_index("ysp")
    space = lax.axis_index("space")
    last = lax.axis_size("space") - 1
    rows = y_ref.shape[1] * ROWS
    for x in range(4):
        y1 = y_ref[x].reshape(rows, MID_L)
        sig = sigmoid(y1)
        slope = sig * (1.0 + y1 * (1.0 - sig)) * plane_mask(x, rows, space, last, core)
        d_ref[x] = slope.reshape(y_ref.shape[1:])


def parity():
    bits = lax.axis_index("ysp")
    for axis in ("dp", "space"):
        at, count = lax.axis_index(axis), lax.axis_size(axis)
        while count > 1:
            bits, at, count = bits + at % 2, at // 2, (count + 1) // 2
    return bits % 2


def halves(pack, which):
    count = pack.shape[0] // 2
    return pack[pl.ds(which * count, count), :], pack[pl.ds((1 - which) * count, count), :].astype(BF)


def adjoint(wide_ref, taps_ref, tall, wide):
    cells = taps(lambda a, b: wide_ref[2 - a : 2 - a + tall, 2 - b : 2 - b + wide])
    return dot(cells, taps_ref[...].reshape(9 * 384, -1), NN)


def backward_body(g_ref, by_ref, ev_ref, od_ref, r2_ref, d_ref, e_ref, k2_ref, h2_ref, k_ref, s_ref, t_ref, wide_g, acc, pack, pack2):
    core = lax.axis_index("ysp")
    space = lax.axis_index("space")
    spread(gathered(g_ref, by_ref, ev_ref, od_ref, space), core, wide_g, MID_L)
    narrow = g_ref.shape[1]
    wide = narrow + 2
    rows = wide * ROWS
    acc[...] = adjoint(wide_g, r2_ref, 4, wide)
    for x in range(4):
        slope = d_ref[x].reshape(rows, MID_L)
        g1 = (acc[x * rows : (x + 1) * rows, :] * slope).astype(BF)
        t_ref[x] = g1.reshape(wide, ROWS, MID_L)
    g1 = t_ref[1:3, 1 : 1 + narrow].reshape(-1, MID_L)
    turned, bias = flipped(g1)
    lane = lax.broadcasted_iota(jnp.int32, (64, 384), 1)
    none = jnp.zeros((64, 128), F32)
    held = None
    for tap in range(9):
        a, b = divmod(tap, 3)
        cells = e_ref[1 + a : 3 + a, 1 + b : 1 + b + narrow].reshape(-1, 256)
        found = tap_sum(dot(turned, cells, NN), C_IN)
        if tap == 8:
            pack[:, 768:896] = jnp.where(lane < TAP1, jnp.concatenate([found, none], axis=1), bias)[:, :128]
            continue
        found = jnp.concatenate([found, none], axis=1)
        slot = tap % 4
        if slot == 0:
            held = found
        else:
            held = jnp.where(lane < slot * TAP1, held, pltpu.roll(found, slot * TAP1, 1))
        if slot == 3:
            at = (tap - 3) * TAP1
            pack[:, at : at + 384] = held
    which = parity()
    k_ref[:32], s_ref[:32] = halves(pack, which)
    pack2[...] = k2_ref[...] + h2_ref[...].astype(F32)
    keep, send = halves(pack2, which)
    k_ref[32:48], k_ref[48:] = keep[:, :PACK1], keep[:, PACK1:]
    s_ref[32:48], s_ref[48:] = send[:, :PACK1], send[:, PACK1:]


def input_grad_body(t_ref, r1_ref, o_ref, wide_g):
    for x in range(t_ref.shape[0]):
        wide_g[x, :, :, :MID_L] = t_ref[x]
        edge = edges(t_ref[x].reshape(-1, MID_L).astype(F32), 0, 128)
        wide_g[x, :, :, MID_L:] = edge.astype(BF).reshape(-1, ROWS, 128)
    o_ref[...] = adjoint(wide_g, r1_ref, *o_ref.shape[:2]).astype(BF).reshape(o_ref.shape)


def finish_body(m_ref, h_ref, w2_ref, b2_ref, w1_ref, b1_ref, pack2, pack1):
    which = parity()
    first = lax.axis_index("dp") % 2
    for ref, of in ((m_ref, which), (h_ref, 1 - which)):
        for at, half in ((0, first), (32, 1 - first)):
            rows = pl.ds(half * 32 + of * 16, 16)
            pack2[rows, :PACK1] = ref[at : at + 16].astype(F32)
            pack2[rows, PACK1:] = ref[at + 16 : at + 32].astype(F32)
        pack1[pl.ds(of * 32, 32), :] = ref[64:].astype(F32)
    row = lax.broadcasted_iota(jnp.int32, (64, 64), 0)
    col = lax.broadcasted_iota(jnp.int32, (64, 64), 1)
    for pack, w_ref, b_ref in ((pack2, w2_ref, b2_ref), (pack1, w1_ref, b1_ref)):
        width = w_ref.shape[1]
        w_ref[...] = pack[:, :width]
        spot = jnp.broadcast_to(pack[:, width : width + 1], (64, 64))
        b_ref[...] = jnp.sum(jnp.where(row == col, spot, 0.0), axis=0, keepdims=True)


def swap(cells, axis, bit):
    return lax.ppermute(cells, axis, [(i, i ^ bit) for i in range(lax.axis_size(axis))])


def halo(own, edge, *ready):
    side, *ready = hold((swap(edge, "ysp", 1), *ready))
    cells = jnp.concatenate([own, side], axis=1)
    count = lax.axis_size("space")
    pairs = [(i, i + 1) for i in range(1, count - 1, 2)]
    odd = lax.ppermute(cells, "space", pairs + [(j, i) for i, j in pairs])
    pairs = [(i, i + 1) for i in range(0, count - 1, 2)]
    even = lax.ppermute(cells, "space", pairs + [(j, i) for i, j in pairs])
    return side, even, odd, *ready


def powers(axis, first):
    return [m for m in (1, 2, 4, 8, 16, 32, 64) if first <= m < lax.axis_size(axis)]


def cross(cells, axis, bit):
    pairs = [(2 * i + c, 2 * (i ^ bit) + 1 - c) for i in range(lax.axis_size(axis)) for c in range(2)]
    return lax.ppermute(cells, (axis, "ysp"), pairs)


def on_device(inputs, w_first, b_first, w_second, b_second, cotangent):
    nx, ny = inputs.shape[1], inputs.shape[2]
    own = inputs.reshape(nx, ny, ROWS, IN_L)
    edge = lax.dynamic_slice_in_dim(own, (1 - lax.axis_index("ysp")) * (ny - 2), 2, axis=1)
    side, even, odd = halo(own, edge)
    hbm = pl.BlockSpec(memory_space=pltpu.HBM)
    banded = call(
        banded_body,
        2000000000,
        [
            ((256, 9 * 256), BF),
            ((256, 9 * 384), BF),
            ((9, 384, 256), BF),
            ((9, 384, 128), BF),
            ((2, MID_L), F32),
        ],
        [
            pltpu.VMEM((64, W1_L), F32),
            pltpu.VMEM((64, W2_L), F32),
            pltpu.VMEM((2, C_MID), F32),
            pltpu.SemaphoreType.DMA((4,)),
        ],
        vmem=16 << 20,
        in_specs=[hbm] * 4,
    )(*[pltpu.with_memory_space_constraint(v, pltpu.HBM) for v in (w_first.T, w_second.T, b_first.reshape(1, C_MID), b_second.reshape(1, C_MID))])
    cot = cotangent.reshape(nx, ny, ROWS, MID_L)
    even, odd, cot, f1, f2, r2, r1, bias = hold((even, odd, cot, *banded))
    wide_in, act, y1, out, g2, edge = call(
        forward_body,
        4800000000,
        [
            ((nx + 4, ny + 4, ROWS, 256), BF),
            ((nx + 2, ny + 2, ROWS, 384), BF),
            ((nx + 2, ny + 2, ROWS, MID_L), F32),
            ((nx, ny, ROWS, MID_L), BF),
            ((nx, ny, ROWS, MID_L), BF),
            ((nx, 2, ROWS, MID_L), BF),
        ],
        [pltpu.VMEM(((nx + 2) * (ny + 2) * ROWS, MID_L), F32)],
    )(own, side, even, odd, f1, f2, bias, cot)
    keep2, send2, slope = call(
        second_weights_body,
        1800000000,
        [((32, PACK2), F32), ((32, PACK2), BF), ((nx + 2, ny + 2, ROWS, MID_L), F32)],
        [pltpu.VMEM((64, PACK2), F32)],
    )(act, g2, y1)
    side, even, odd, keep2, send2, slope = halo(g2, edge, keep2, send2, slope)
    got2 = cross(send2, "dp", 1)
    even, odd, keep2, got2 = hold((even, odd, keep2, got2))
    keep, send, g1 = call(
        backward_body,
        5600000000,
        [((64, PACK1), F32), ((64, PACK1), BF), ((nx + 2, ny + 2, ROWS, MID_L), BF)],
        [
            pltpu.VMEM((nx + 4, ny + 4, ROWS, 384), BF),
            pltpu.VMEM(((nx + 2) * (ny + 2) * ROWS, MID_L), F32),
            pltpu.VMEM((64, PACK1), F32),
            pltpu.VMEM((32, PACK2), F32),
        ],
    )(g2, side, even, odd, r2, slope, wide_in, keep2, got2)
    total = hold((keep + swap(send, "ysp", 1).astype(F32)).astype(BF))
    sum1, sum2 = hold((total[:32], total[32:]))
    (d_in,) = call(
        input_grad_body,
        1200000000,
        [((nx, ny, ROWS, IN_L), BF)],
        [pltpu.VMEM((nx + 2, ny + 2, ROWS, 384), BF)],
    )(g1, r1)
    output = out.reshape(1, nx, ny, DEPTH * C_MID)
    input_grad = d_in.reshape(1, nx, ny, DEPTH * C_IN)
    along = [("space", m) for m in powers("space", 1)]
    stages1 = [("dp", m) for m in powers("dp", 1)] + along
    stages2 = [("dp", m) for m in powers("dp", 2)] + along
    for at, (one, two) in enumerate(zip(stages1, [*stages2, None])):
        got1 = cross(sum1, *one)
        got2 = cross(sum2, *(two or ("dp", 1)))
        if at == 2:
            got1, output = hold((got1, output))
        if at == 2:
            got1, input_grad = hold((got1, input_grad))
        sum1 = hold(sum1 + got1)
        if two:
            sum2 = hold(sum2 + got2)
    total = jnp.concatenate([sum2, got2, sum1], axis=0)
    gw2, gb2, gw1, gb1 = call(
        finish_body,
        1200000000,
        [((64, W2_L), F32), ((1, 64), F32), ((64, W1_L), F32), ((1, 64), F32)],
        [pltpu.VMEM((64, PACK2), F32), pltpu.VMEM((64, PACK1), F32)],
    )(total, swap(total, "ysp", 1))
    return (output, input_grad, gw1.T, gb1.reshape(64), gw2.T, gb2.reshape(64))


def solution(mesh):
    placed = P(("groups", "dp"), "space", "ysp", None)
    return jax.shard_map(
        on_device,
        mesh=mesh,
        in_specs=(placed, P(), P(), P(), P(), placed),
        out_specs=(placed, placed, P("groups", None), P("groups"), P("groups", None), P("groups")),
        check_vma=False,
    )
```

```python
import jax
import jax.numpy as jnp
from jax import lax
from jax.experimental import pallas as pl
from jax.experimental.pallas import tpu as pltpu
from jax.sharding import PartitionSpec as P

C_IN = 32
C_MID = 64
DEPTH = 64
BF = jnp.bfloat16
F32 = jnp.float32
hold = lax.optimization_barrier
GROUP = 4
ROWS = DEPTH // GROUP
IN_L = GROUP * C_IN
MID_L = GROUP * C_MID
TAP1 = 3 * C_IN
TAP2 = 3 * C_MID
W1_L = 9 * TAP1
W2_L = 9 * TAP2
PACK2 = 1792
PACK1 = 896
NT = (((1,), (1,)), ((), ()))
NN = (((1,), (0,)), ((), ()))


def call(body, flops, outs, scratch=(), vmem=16 << 20, **specs):
    return pl.pallas_call(
        body,
        out_shape=[jax.ShapeDtypeStruct(shape, kind) for shape, kind in outs],
        scratch_shapes=list(scratch),
        compiler_params=pltpu.CompilerParams(vmem_limit_bytes=vmem),
        cost_estimate=pl.CostEstimate(flops=flops, bytes_accessed=flops // 256, transcendentals=0),
        **specs,
    )


def dot(a, b, dims):
    return lax.dot_general(a, b, dims, preferred_element_type=F32)


def window(ref, start, width):
    frame = 256 if width <= 128 else 384
    at = start // 128 * 128
    stop = min(at + frame, ref.shape[1])
    value = ref[:, at:stop]
    if stop < at + frame:
        value = jnp.concatenate([value, jnp.zeros((64, at + frame - stop), F32)], axis=1)
    if start != at:
        value = pltpu.roll(value, frame - (start - at), 1)
    lane = lax.broadcasted_iota(jnp.int32, value.shape, 1)
    return jnp.where(lane < width, value, 0.0)


def banded_body(w1_ref, w2_ref, b1_ref, b2_ref, f1_ref, f2_ref, r2_ref, r1_ref, bias_ref, pad1, pad2, lines, sems):
    copies = [
        pltpu.make_async_copy(w1_ref, pad1, sems.at[0]),
        pltpu.make_async_copy(w2_ref, pad2, sems.at[1]),
        pltpu.make_async_copy(b1_ref, lines.at[pl.ds(0, 1)], sems.at[2]),
        pltpu.make_async_copy(b2_ref, lines.at[pl.ds(1, 1)], sems.at[3]),
    ]
    for copy in copies:
        copy.start()
    for copy in copies:
        copy.wait()
    bias_ref[...] = jnp.concatenate([lines[...]] * GROUP, axis=1)
    for tap in range(9):
        one = window(pad1, tap * TAP1, TAP1)
        two = window(pad2, tap * TAP2, TAP2)
        for m in range(-1, 5):
            at = (m % 6) * C_MID
            s1 = pltpu.roll(one, ((m - 1) * C_IN) % 256, 1) if m != 1 else one
            s2 = pltpu.roll(two, ((m - 1) * C_MID) % 384, 1) if m != 1 else two
            s1 = s1.astype(BF)
            s2 = s2.astype(BF)
            if 0 <= m < 4:
                f1_ref[m * C_MID : (m + 1) * C_MID, tap * 256 : (tap + 1) * 256] = s1
                f2_ref[m * C_MID : (m + 1) * C_MID, tap * 384 : (tap + 1) * 384] = s2
            r1_ref[tap, at : at + C_MID, :] = s1[:, :IN_L]
            r2_ref[tap, at : at + C_MID, :] = s2[:, :MID_L]


def edges(value, low, high):
    count = value.shape[0]
    row = lax.broadcasted_iota(jnp.int32, (count, 128), 0) % ROWS
    lane = lax.broadcasted_iota(jnp.int32, (count, 128), 1)
    after = pltpu.roll(value[:, low : low + 128], count - 1, 0)
    before = pltpu.roll(value[:, high : high + 128], 1, 0)
    after = jnp.where(row == ROWS - 1, 0.0, after)
    before = jnp.where(row == 0, 0.0, before)
    return jnp.where(lane < 64, after, before)


def spread(parts, core, to_ref, lanes):
    for x, (middle, side) in enumerate(parts):
        side = side.astype(F32)
        low = jnp.where(core == 1, side, 0.0)
        high = jnp.where(core == 0, side, 0.0)
        cells = jnp.concatenate([low, middle.astype(F32), high], axis=0)
        rows = cells.reshape(-1, lanes)
        shape = cells.shape[:2]
        to_ref[x, :, :, :lanes] = cells.astype(BF)
        edge = edges(rows, 0, lanes - 128)
        to_ref[x, :, :, lanes:] = edge.astype(BF).reshape(*shape, 128)


def gathered(own, side, even, odd, space):
    count, narrow = own.shape[:2]
    both = [(even[i], odd[i]) for i in range(even.shape[0])]
    flip = space % 2 == 1
    left = [jnp.where(flip, one, two) for one, two in both]
    right = [jnp.where(flip, two, one) for one, two in both]
    mid = [(own[i], side[i]) for i in range(count)]
    return [(p[:narrow], p[narrow:]) for p in left] + mid + [(p[:narrow], p[narrow:]) for p in right]


def taps(of):
    parts = [of(*divmod(tap, 3)) for tap in range(9)]
    return jnp.concatenate([part.reshape(-1, part.shape[-1]) for part in parts], axis=1)


def sigmoid(value):
    return 0.5 * jnp.tanh(0.5 * value) + 0.5


def plane_mask(x, rows, space, last, core):
    row = lax.broadcasted_iota(jnp.int32, (rows, 1), 0)
    inside = jnp.float32(1.0)
    if x == 0:
        inside = jnp.where(space > 0, 1.0, 0.0)
    if x == 3:
        inside = jnp.where(space < last, 1.0, 0.0)
    low = jnp.where(core == 1, 1.0, 0.0)
    high = jnp.where(core == 0, 1.0, 0.0)
    mask = jnp.where(row < ROWS, low, jnp.where(row >= rows - ROWS, high, 1.0))
    return mask * inside


def forward_body(x_ref, by_ref, ev_ref, od_ref, f1_ref, f2_ref, b_ref, c_ref, e_ref, a_ref, d_ref, o_ref, g_ref, n_ref, acc):
    core = lax.axis_index("ysp")
    space = lax.axis_index("space")
    last = lax.axis_size("space") - 1
    spread(gathered(x_ref, by_ref, ev_ref, od_ref, space), core, e_ref, IN_L)
    wide = x_ref.shape[1] + 2
    narrow = wide - 2
    acc[...] = dot(taps(lambda a, b: e_ref[a : a + 4, b : b + wide]), f1_ref[...], NT)
    rows = wide * ROWS
    bias1, bias2 = b_ref[0:1], b_ref[1:2]
    for x in range(4):
        y1 = acc[x * rows : (x + 1) * rows, :] + bias1
        mask = plane_mask(x, rows, space, last, core)
        sig = sigmoid(y1)
        d_ref[x] = y1.reshape(wide, ROWS, MID_L)
        act = (y1 * sig * mask).astype(BF)
        a_ref[x, :, :, :MID_L] = act.reshape(wide, ROWS, MID_L)
        edge = edges(act.astype(F32), 0, 128)
        a_ref[x, :, :, MID_L:] = edge.astype(BF).reshape(wide, ROWS, 128)
    y2 = dot(taps(lambda a, b: a_ref[a : a + 2, b : b + narrow]), f2_ref[...], NT) + bias2
    sig = sigmoid(y2)
    shape = o_ref.shape
    o_ref[...] = (y2 * sig).astype(BF).reshape(shape)
    cot = c_ref[...].reshape(-1, MID_L).astype(F32)
    g_ref[...] = (cot * (sig * (1.0 + y2 * (1.0 - sig)))).astype(BF).reshape(shape)
    n_ref[...] = g_ref[:, pl.ds((1 - core) * (narrow - 2), 2)]


def flipped(grads):
    turned = grads.astype(F32).T
    sums = jnp.sum(turned, axis=1, keepdims=True)
    bias = sums[0:64] + sums[64:128] + sums[128:192] + sums[192:256]
    return turned.astype(BF), bias


def tap_sum(product, step):
    frame = product.shape[1]
    total = product[64:128]
    for j in (0, 2, 3):
        total = total + pltpu.roll(product[j * 64 : (j + 1) * 64], (frame - (j - 1) * step) % frame, 1)
    return total


def second_weights_body(a_ref, g_ref, y_ref, k_ref, s_ref, d_ref, p_ref):
    turned, bias = flipped(g_ref[...].reshape(-1, MID_L))
    narrow = g_ref.shape[1]
    lane = lax.broadcasted_iota(jnp.int32, (64, 384), 1)
    held = None
    for tap in range(9):
        a, b = divmod(tap, 3)
        found = tap_sum(dot(turned, a_ref[a : a + 2, b : b + narrow].reshape(-1, 384), NN), C_MID)
        if tap == 8:
            p_ref[:, 1536:1792] = jnp.where(lane < TAP2, found, bias)[:, :256]
        elif tap % 2 == 0:
            held = found
        else:
            at = (tap - 1) * TAP2
            p_ref[:, at : at + 384] = jnp.where(lane < TAP2, held, pltpu.roll(found, TAP2, 1))
    k_ref[...], s_ref[...] = halves(p_ref, lax.axis_index("dp") % 2)
    core = lax.axis_index("ysp")
    space = lax.axis_index("space")
    last = lax.axis_size("space") - 1
    rows = y_ref.shape[1] * ROWS
    for x in range(4):
        y1 = y_ref[x].reshape(rows, MID_L)
        sig = sigmoid(y1)
        slope = sig * (1.0 + y1 * (1.0 - sig)) * plane_mask(x, rows, space, last, core)
        d_ref[x] = slope.reshape(y_ref.shape[1:])


def parity():
    bits = lax.axis_index("ysp")
    for axis in ("dp", "space"):
        at, count = lax.axis_index(axis), lax.axis_size(axis)
        while count > 1:
            bits, at, count = bits + at % 2, at // 2, (count + 1) // 2
    return bits % 2


def halves(pack, which):
    count = pack.shape[0] // 2
    return pack[pl.ds(which * count, count), :], pack[pl.ds((1 - which) * count, count), :].astype(BF)


def adjoint(wide_ref, taps_ref, tall, wide):
    cells = taps(lambda a, b: wide_ref[2 - a : 2 - a + tall, 2 - b : 2 - b + wide])
    return dot(cells, taps_ref[...].reshape(9 * 384, -1), NN)


def backward_body(g_ref, by_ref, ev_ref, od_ref, r2_ref, d_ref, e_ref, k2_ref, h2_ref, k_ref, s_ref, t_ref, wide_g, pack, pack2):
    core = lax.axis_index("ysp")
    space = lax.axis_index("space")
    near = gathered(g_ref, by_ref, ev_ref, od_ref, space)[1:5]
    spread([(middle, jnp.where(core == 0, side[:1], side[1:])) for middle, side in near], core, wide_g, MID_L)
    narrow = g_ref.shape[1]
    slope = d_ref[1:3, 1 : 1 + narrow].reshape(-1, MID_L)
    g1 = (adjoint(wide_g, r2_ref, 2, narrow) * slope).astype(BF)
    t_ref[...] = g1.reshape(t_ref.shape)
    turned, bias = flipped(g1)
    lane = lax.broadcasted_iota(jnp.int32, (64, 384), 1)
    none = jnp.zeros((64, 128), F32)
    held = None
    for tap in range(9):
        a, b = divmod(tap, 3)
        cells = e_ref[1 + a : 3 + a, 1 + b : 1 + b + narrow].reshape(-1, 256)
        found = tap_sum(dot(turned, cells, NN), C_IN)
        if tap == 8:
            pack[:, 768:896] = jnp.where(lane < TAP1, jnp.concatenate([found, none], axis=1), bias)[:, :128]
            continue
        found = jnp.concatenate([found, none], axis=1)
        slot = tap % 4
        if slot == 0:
            held = found
        else:
            held = jnp.where(lane < slot * TAP1, held, pltpu.roll(found, slot * TAP1, 1))
        if slot == 3:
            at = (tap - 3) * TAP1
            pack[:, at : at + 384] = held
    which = parity()
    k_ref[:32], s_ref[:32] = halves(pack, which)
    pack2[...] = k2_ref[...] + h2_ref[...].astype(F32)
    keep, send = halves(pack2, which)
    k_ref[32:48], k_ref[48:] = keep[:, :PACK1], keep[:, PACK1:]
    s_ref[32:48], s_ref[48:] = send[:, :PACK1], send[:, PACK1:]


def outer_body(g_ref, by_ref, ev_ref, od_ref, r2_ref, d_ref, t_ref, o_ref, wide_g):
    core = lax.axis_index("ysp")
    space = lax.axis_index("space")
    spread(gathered(g_ref, by_ref, ev_ref, od_ref, space), core, wide_g, MID_L)
    narrow = g_ref.shape[1]
    wide = narrow + 2
    at = (1 - core) * (wide - 1)

    def around(a, b):
        cols = pl.ds(2 - b, wide)
        beside = wide_g[3 - a : 5 - a, pl.ds(2 - b + at, 1)]
        return jnp.concatenate([wide_g[2 - a, cols], wide_g[5 - a, cols], beside[:, 0]], axis=0)

    slope = jnp.concatenate([d_ref[0], d_ref[3], d_ref[1:3, pl.ds(at, 1)][:, 0]], axis=0)
    g1 = dot(taps(around), r2_ref[...].reshape(9 * 384, -1), NN) * slope.reshape(-1, MID_L)
    g1 = g1.astype(BF).reshape(-1, ROWS, MID_L)
    none = jnp.zeros((1, ROWS, MID_L), BF)
    planes = [g1[:wide], None, None, g1[wide : 2 * wide]]
    for x in (1, 2):
        other = g1[2 * wide + x - 1 : 2 * wide + x]
        low = jnp.where(core == 1, other, none)
        high = jnp.where(core == 0, other, none)
        planes[x] = jnp.concatenate([low, t_ref[x - 1], high], axis=0)
    for x in range(4):
        o_ref[x, :, :, :MID_L] = planes[x]
        edge = edges(planes[x].reshape(-1, MID_L).astype(F32), 0, 128)
        o_ref[x, :, :, MID_L:] = edge.astype(BF).reshape(wide, ROWS, 128)


def input_grad_body(t_ref, r1_ref, o_ref):
    o_ref[...] = adjoint(t_ref, r1_ref, *o_ref.shape[:2]).astype(BF).reshape(o_ref.shape)


def finish_body(m_ref, h_ref, w2_ref, b2_ref, w1_ref, b1_ref, pack2, pack1):
    which = parity()
    first = lax.axis_index("dp") % 2
    for ref, of in ((m_ref, which), (h_ref, 1 - which)):
        for at, half in ((0, first), (32, 1 - first)):
            rows = pl.ds(half * 32 + of * 16, 16)
            pack2[rows, :PACK1] = ref[at : at + 16].astype(F32)
            pack2[rows, PACK1:] = ref[at + 16 : at + 32].astype(F32)
        pack1[pl.ds(of * 32, 32), :] = ref[64:].astype(F32)
    row = lax.broadcasted_iota(jnp.int32, (64, 64), 0)
    col = lax.broadcasted_iota(jnp.int32, (64, 64), 1)
    for pack, w_ref, b_ref in ((pack2, w2_ref, b2_ref), (pack1, w1_ref, b1_ref)):
        width = w_ref.shape[1]
        w_ref[...] = pack[:, :width]
        spot = jnp.broadcast_to(pack[:, width : width + 1], (64, 64))
        b_ref[...] = jnp.sum(jnp.where(row == col, spot, 0.0), axis=0, keepdims=True)


def swap(cells, axis, bit):
    return lax.ppermute(cells, axis, [(i, i ^ bit) for i in range(lax.axis_size(axis))])


def halo(own, edge, *ready):
    side, *ready = hold((swap(edge, "ysp", 1), *ready))
    cells = jnp.concatenate([own, side], axis=1)
    count = lax.axis_size("space")
    pairs = [(i, i + 1) for i in range(1, count - 1, 2)]
    odd = lax.ppermute(cells, "space", pairs + [(j, i) for i, j in pairs])
    pairs = [(i, i + 1) for i in range(0, count - 1, 2)]
    even = lax.ppermute(cells, "space", pairs + [(j, i) for i, j in pairs])
    return side, even, odd, *ready


def powers(axis, first):
    return [m for m in (1, 2, 4, 8, 16, 32, 64) if first <= m < lax.axis_size(axis)]


def cross(cells, axis, bit):
    pairs = [(2 * i + c, 2 * (i ^ bit) + 1 - c) for i in range(lax.axis_size(axis)) for c in range(2)]
    return lax.ppermute(cells, (axis, "ysp"), pairs)


def on_device(inputs, w_first, b_first, w_second, b_second, cotangent):
    nx, ny = inputs.shape[1], inputs.shape[2]
    own = inputs.reshape(nx, ny, ROWS, IN_L)
    edge = lax.dynamic_slice_in_dim(own, (1 - lax.axis_index("ysp")) * (ny - 2), 2, axis=1)
    side, even, odd = halo(own, edge)
    hbm = pl.BlockSpec(memory_space=pltpu.HBM)
    banded = call(
        banded_body,
        2000000000,
        [
            ((256, 9 * 256), BF),
            ((256, 9 * 384), BF),
            ((9, 384, 256), BF),
            ((9, 384, 128), BF),
            ((2, MID_L), F32),
        ],
        [
            pltpu.VMEM((64, W1_L), F32),
            pltpu.VMEM((64, W2_L), F32),
            pltpu.VMEM((2, C_MID), F32),
            pltpu.SemaphoreType.DMA((4,)),
        ],
        vmem=16 << 20,
        in_specs=[hbm] * 4,
    )(*[pltpu.with_memory_space_constraint(v, pltpu.HBM) for v in (w_first.T, w_second.T, b_first.reshape(1, C_MID), b_second.reshape(1, C_MID))])
    cot = cotangent.reshape(nx, ny, ROWS, MID_L)
    even, odd, cot, f1, f2, r2, r1, bias = hold((even, odd, cot, *banded))
    wide_in, act, y1, out, g2, edge = call(
        forward_body,
        4800000000,
        [
            ((nx + 4, ny + 4, ROWS, 256), BF),
            ((nx + 2, ny + 2, ROWS, 384), BF),
            ((nx + 2, ny + 2, ROWS, MID_L), F32),
            ((nx, ny, ROWS, MID_L), BF),
            ((nx, ny, ROWS, MID_L), BF),
            ((nx, 2, ROWS, MID_L), BF),
        ],
        [pltpu.VMEM(((nx + 2) * (ny + 2) * ROWS, MID_L), F32)],
    )(own, side, even, odd, f1, f2, bias, cot)
    keep2, send2, slope = call(
        second_weights_body,
        1800000000,
        [((32, PACK2), F32), ((32, PACK2), BF), ((nx + 2, ny + 2, ROWS, MID_L), F32)],
        [pltpu.VMEM((64, PACK2), F32)],
    )(act, g2, y1)
    side, even, odd, keep2, send2, slope = halo(g2, edge, keep2, send2, slope)
    got2 = cross(send2, "dp", 1)
    even, odd, keep2, got2 = hold((even, odd, keep2, got2))
    keep, send, g1 = call(
        backward_body,
        5600000000,
        [((64, PACK1), F32), ((64, PACK1), BF), ((nx, ny, ROWS, MID_L), BF)],
        [
            pltpu.VMEM((nx + 2, ny + 2, ROWS, 384), BF),
            pltpu.VMEM((64, PACK1), F32),
            pltpu.VMEM((32, PACK2), F32),
        ],
    )(g2, side, even, odd, r2, slope, wide_in, keep2, got2)
    total = hold((keep + swap(send, "ysp", 1).astype(F32)).astype(BF))
    sum1, sum2 = hold((total[:32], total[32:]))
    (wide_g,) = call(
        outer_body,
        1400000000,
        [((nx + 2, ny + 2, ROWS, 384), BF)],
        [pltpu.VMEM((nx + 4, ny + 4, ROWS, 384), BF)],
    )(g2, side, even, odd, r2, slope, g1)
    output = out.reshape(1, nx, ny, DEPTH * C_MID)
    along = [("space", m) for m in powers("space", 1)]
    stages1 = [("dp", m) for m in powers("dp", 1)] + along
    stages2 = [("dp", m) for m in powers("dp", 2)] + along
    for at, (one, two) in enumerate(zip(stages1, [*stages2, None])):
        got1 = cross(sum1, *one)
        got2 = cross(sum2, *(two or ("dp", 1)))
        if at == 0:
            got1, wide_g = hold((got1, wide_g))
            (d_in,) = call(input_grad_body, 1200000000, [((nx, ny, ROWS, IN_L), BF)])(wide_g, r1)
            input_grad = d_in.reshape(1, nx, ny, DEPTH * C_IN)
        if at == 2:
            got1, output = hold((got1, output))
        if at == 2:
            got1, input_grad = hold((got1, input_grad))
        sum1 = hold(sum1 + got1)
        if two:
            sum2 = hold(sum2 + got2)
    total = jnp.concatenate([sum2, got2, sum1], axis=0)
    gw2, gb2, gw1, gb1 = call(
        finish_body,
        1200000000,
        [((64, W2_L), F32), ((1, 64), F32), ((64, W1_L), F32), ((1, 64), F32)],
        [pltpu.VMEM((64, PACK2), F32), pltpu.VMEM((64, PACK1), F32)],
    )(total, swap(total, "ysp", 1))
    return (output, input_grad, gw1.T, gb1.reshape(64), gw2.T, gb2.reshape(64))


def solution(mesh):
    placed = P(("groups", "dp"), "space", "ysp", None)
    return jax.shard_map(
        on_device,
        mesh=mesh,
        in_specs=(placed, P(), P(), P(), P(), placed),
        out_specs=(placed, placed, P("groups", None), P("groups"), P("groups", None), P("groups")),
        check_vma=False,
    )
```

```python
import jax
import jax.numpy as jnp
from jax import lax
from jax.experimental import pallas as pl
from jax.experimental.pallas import tpu as pltpu
from jax.sharding import PartitionSpec as P

C_IN = 32
C_MID = 64
DEPTH = 64
BF = jnp.bfloat16
F32 = jnp.float32
hold = lax.optimization_barrier
GROUP = 4
ROWS = DEPTH // GROUP
IN_L = GROUP * C_IN
MID_L = GROUP * C_MID
TAP1 = 3 * C_IN
TAP2 = 3 * C_MID
W1_L = 9 * TAP1
W2_L = 9 * TAP2
PACK2 = 1792
PACK1 = 896
NT = (((1,), (1,)), ((), ()))
NN = (((1,), (0,)), ((), ()))


def call(body, flops, outs, scratch=(), vmem=16 << 20, **specs):
    return pl.pallas_call(
        body,
        out_shape=[jax.ShapeDtypeStruct(shape, kind) for shape, kind in outs],
        scratch_shapes=list(scratch),
        compiler_params=pltpu.CompilerParams(vmem_limit_bytes=vmem),
        cost_estimate=pl.CostEstimate(flops=flops, bytes_accessed=flops // 256, transcendentals=0),
        **specs,
    )


def dot(a, b, dims):
    return lax.dot_general(a, b, dims, preferred_element_type=F32)


def window(ref, start, width):
    frame = 256 if width <= 128 else 384
    at = start // 128 * 128
    stop = min(at + frame, ref.shape[1])
    value = ref[:, at:stop]
    if stop < at + frame:
        value = jnp.concatenate([value, jnp.zeros((64, at + frame - stop), F32)], axis=1)
    if start != at:
        value = pltpu.roll(value, frame - (start - at), 1)
    lane = lax.broadcasted_iota(jnp.int32, value.shape, 1)
    return jnp.where(lane < width, value, 0.0)


def banded_body(w1_ref, w2_ref, b1_ref, b2_ref, f1_ref, f2_ref, r2_ref, r1_ref, bias_ref, pad1, pad2, lines, sems):
    copies = [
        pltpu.make_async_copy(w1_ref, pad1, sems.at[0]),
        pltpu.make_async_copy(w2_ref, pad2, sems.at[1]),
        pltpu.make_async_copy(b1_ref, lines.at[pl.ds(0, 1)], sems.at[2]),
        pltpu.make_async_copy(b2_ref, lines.at[pl.ds(1, 1)], sems.at[3]),
    ]
    for copy in copies:
        copy.start()
    for copy in copies:
        copy.wait()
    bias_ref[...] = jnp.concatenate([lines[...]] * GROUP, axis=1)
    for tap in range(9):
        one = window(pad1, tap * TAP1, TAP1)
        two = window(pad2, tap * TAP2, TAP2)
        for m in range(-1, 5):
            at = (m % 6) * C_MID
            s1 = pltpu.roll(one, ((m - 1) * C_IN) % 256, 1) if m != 1 else one
            s2 = pltpu.roll(two, ((m - 1) * C_MID) % 384, 1) if m != 1 else two
            s1 = s1.astype(BF)
            s2 = s2.astype(BF)
            if 0 <= m < 4:
                f1_ref[m * C_MID : (m + 1) * C_MID, tap * 256 : (tap + 1) * 256] = s1
                f2_ref[m * C_MID : (m + 1) * C_MID, tap * 384 : (tap + 1) * 384] = s2
            r1_ref[tap, at : at + C_MID, :] = s1[:, :IN_L]
            r2_ref[tap, at : at + C_MID, :] = s2[:, :MID_L]


def edges(value, low, high):
    count = value.shape[0]
    row = lax.broadcasted_iota(jnp.int32, (count, 128), 0) % ROWS
    lane = lax.broadcasted_iota(jnp.int32, (count, 128), 1)
    after = pltpu.roll(value[:, low : low + 128], count - 1, 0)
    before = pltpu.roll(value[:, high : high + 128], 1, 0)
    after = jnp.where(row == ROWS - 1, 0.0, after)
    before = jnp.where(row == 0, 0.0, before)
    return jnp.where(lane < 64, after, before)


def spread(parts, core, to_ref, lanes):
    for x, (middle, side) in enumerate(parts):
        side = side.astype(F32)
        low = jnp.where(core == 1, side, 0.0)
        high = jnp.where(core == 0, side, 0.0)
        cells = jnp.concatenate([low, middle.astype(F32), high], axis=0)
        rows = cells.reshape(-1, lanes)
        shape = cells.shape[:2]
        to_ref[x, :, :, :lanes] = cells.astype(BF)
        edge = edges(rows, 0, lanes - 128)
        to_ref[x, :, :, lanes:] = edge.astype(BF).reshape(*shape, 128)


def gathered(own, side, even, odd, space):
    count, narrow = own.shape[:2]
    both = [(even[i], odd[i]) for i in range(even.shape[0])]
    flip = space % 2 == 1
    left = [jnp.where(flip, one, two) for one, two in both]
    right = [jnp.where(flip, two, one) for one, two in both]
    mid = [(own[i], side[i]) for i in range(count)]
    return [(p[:narrow], p[narrow:]) for p in left] + mid + [(p[:narrow], p[narrow:]) for p in right]


def taps(of):
    parts = [of(*divmod(tap, 3)) for tap in range(9)]
    return jnp.concatenate([part.reshape(-1, part.shape[-1]) for part in parts], axis=1)


def sigmoid(value):
    return 0.5 * jnp.tanh(0.5 * value) + 0.5


def plane_mask(x, rows, space, last, core):
    row = lax.broadcasted_iota(jnp.int32, (rows, 1), 0)
    inside = jnp.float32(1.0)
    if x == 0:
        inside = jnp.where(space > 0, 1.0, 0.0)
    if x == 3:
        inside = jnp.where(space < last, 1.0, 0.0)
    low = jnp.where(core == 1, 1.0, 0.0)
    high = jnp.where(core == 0, 1.0, 0.0)
    mask = jnp.where(row < ROWS, low, jnp.where(row >= rows - ROWS, high, 1.0))
    return mask * inside


def forward_body(x_ref, by_ref, ev_ref, od_ref, f1_ref, f2_ref, b_ref, c_ref, e_ref, a_ref, d_ref, o_ref, g_ref, n_ref, acc):
    core = lax.axis_index("ysp")
    space = lax.axis_index("space")
    last = lax.axis_size("space") - 1
    spread(gathered(x_ref, by_ref, ev_ref, od_ref, space), core, e_ref, IN_L)
    wide = x_ref.shape[1] + 2
    narrow = wide - 2
    acc[...] = dot(taps(lambda a, b: e_ref[a : a + 4, b : b + wide]), f1_ref[...], NT)
    rows = wide * ROWS
    bias1, bias2 = b_ref[0:1], b_ref[1:2]
    for x in range(4):
        y1 = acc[x * rows : (x + 1) * rows, :] + bias1
        mask = plane_mask(x, rows, space, last, core)
        sig = sigmoid(y1)
        d_ref[x] = y1.reshape(wide, ROWS, MID_L)
        act = (y1 * sig * mask).astype(BF)
        a_ref[x, :, :, :MID_L] = act.reshape(wide, ROWS, MID_L)
        edge = edges(act.astype(F32), 0, 128)
        a_ref[x, :, :, MID_L:] = edge.astype(BF).reshape(wide, ROWS, 128)
    y2 = dot(taps(lambda a, b: a_ref[a : a + 2, b : b + narrow]), f2_ref[...], NT) + bias2
    sig = sigmoid(y2)
    shape = o_ref.shape
    o_ref[...] = (y2 * sig).astype(BF).reshape(shape)
    cot = c_ref[...].reshape(-1, MID_L).astype(F32)
    g_ref[...] = (cot * (sig * (1.0 + y2 * (1.0 - sig)))).astype(BF).reshape(shape)
    n_ref[...] = g_ref[:, pl.ds((1 - core) * (narrow - 2), 2)]


def flipped(grads):
    turned = grads.astype(F32).T
    sums = jnp.sum(turned, axis=1, keepdims=True)
    bias = sums[0:64] + sums[64:128] + sums[128:192] + sums[192:256]
    return turned.astype(BF), bias


def tap_sum(product, step):
    frame = product.shape[1]
    total = product[64:128]
    for j in (0, 2, 3):
        total = total + pltpu.roll(product[j * 64 : (j + 1) * 64], (frame - (j - 1) * step) % frame, 1)
    return total


def second_weights_body(a_ref, g_ref, y_ref, k_ref, s_ref, d_ref, p_ref):
    turned, bias = flipped(g_ref[...].reshape(-1, MID_L))
    narrow = g_ref.shape[1]
    lane = lax.broadcasted_iota(jnp.int32, (64, 384), 1)
    held = None
    for tap in range(9):
        a, b = divmod(tap, 3)
        found = tap_sum(dot(turned, a_ref[a : a + 2, b : b + narrow].reshape(-1, 384), NN), C_MID)
        if tap == 8:
            p_ref[:, 1536:1792] = jnp.where(lane < TAP2, found, bias)[:, :256]
        elif tap % 2 == 0:
            held = found
        else:
            at = (tap - 1) * TAP2
            p_ref[:, at : at + 384] = jnp.where(lane < TAP2, held, pltpu.roll(found, TAP2, 1))
    k_ref[...], s_ref[...] = halves(p_ref, lax.axis_index("dp") % 2)
    core = lax.axis_index("ysp")
    space = lax.axis_index("space")
    last = lax.axis_size("space") - 1
    rows = y_ref.shape[1] * ROWS
    for x in range(4):
        y1 = y_ref[x].reshape(rows, MID_L)
        sig = sigmoid(y1)
        slope = sig * (1.0 + y1 * (1.0 - sig)) * plane_mask(x, rows, space, last, core)
        d_ref[x] = slope.reshape(y_ref.shape[1:])


def parity():
    bits = lax.axis_index("ysp")
    for axis in ("dp", "space"):
        at, count = lax.axis_index(axis), lax.axis_size(axis)
        while count > 1:
            bits, at, count = bits + at % 2, at // 2, (count + 1) // 2
    return bits % 2


def halves(pack, which):
    count = pack.shape[0] // 2
    return pack[pl.ds(which * count, count), :], pack[pl.ds((1 - which) * count, count), :].astype(BF)


def adjoint(wide_ref, taps_ref, tall, wide):
    cells = taps(lambda a, b: wide_ref[2 - a : 2 - a + tall, 2 - b : 2 - b + wide])
    return dot(cells, taps_ref[...].reshape(9 * 384, -1), NN)


def backward_body(g_ref, by_ref, ev_ref, od_ref, r2_ref, d_ref, e_ref, k2_ref, h2_ref, k_ref, s_ref, t_ref, wide_g, pack, pack2):
    core = lax.axis_index("ysp")
    space = lax.axis_index("space")
    near = gathered(g_ref, by_ref, ev_ref, od_ref, space)[1:5]
    spread([(middle, jnp.where(core == 0, side[:1], side[1:])) for middle, side in near], core, wide_g, MID_L)
    narrow = g_ref.shape[1]
    slope = d_ref[1:3, 1 : 1 + narrow].reshape(-1, MID_L)
    g1 = (adjoint(wide_g, r2_ref, 2, narrow) * slope).astype(BF)
    t_ref[...] = g1.reshape(t_ref.shape)
    turned, bias = flipped(g1)
    lane = lax.broadcasted_iota(jnp.int32, (64, 384), 1)
    none = jnp.zeros((64, 128), F32)
    held = None
    for tap in range(9):
        a, b = divmod(tap, 3)
        cells = e_ref[1 + a : 3 + a, 1 + b : 1 + b + narrow].reshape(-1, 256)
        found = tap_sum(dot(turned, cells, NN), C_IN)
        if tap == 8:
            pack[:, 768:896] = jnp.where(lane < TAP1, jnp.concatenate([found, none], axis=1), bias)[:, :128]
            continue
        found = jnp.concatenate([found, none], axis=1)
        slot = tap % 4
        if slot == 0:
            held = found
        else:
            held = jnp.where(lane < slot * TAP1, held, pltpu.roll(found, slot * TAP1, 1))
        if slot == 3:
            at = (tap - 3) * TAP1
            pack[:, at : at + 384] = held
    which = parity()
    k_ref[:32], s_ref[:32] = halves(pack, which)
    pack2[...] = k2_ref[...] + h2_ref[...].astype(F32)
    keep, send = halves(pack2, which)
    k_ref[32:48], k_ref[48:] = keep[:, :PACK1], keep[:, PACK1:]
    s_ref[32:48], s_ref[48:] = send[:, :PACK1], send[:, PACK1:]


def outer_body(g_ref, by_ref, ev_ref, od_ref, r2_ref, d_ref, t_ref, o_ref, wide_g):
    core = lax.axis_index("ysp")
    space = lax.axis_index("space")
    spread(gathered(g_ref, by_ref, ev_ref, od_ref, space), core, wide_g, MID_L)
    narrow = g_ref.shape[1]
    wide = narrow + 2
    at = (1 - core) * (wide - 1)

    def around(a, b):
        cols = pl.ds(2 - b, wide)
        beside = wide_g[3 - a : 5 - a, pl.ds(2 - b + at, 1)]
        return jnp.concatenate([wide_g[2 - a, cols], wide_g[5 - a, cols], beside[:, 0]], axis=0)

    slope = jnp.concatenate([d_ref[0], d_ref[3], d_ref[1:3, pl.ds(at, 1)][:, 0]], axis=0)
    g1 = dot(taps(around), r2_ref[...].reshape(9 * 384, -1), NN) * slope.reshape(-1, MID_L)
    g1 = g1.astype(BF).reshape(-1, ROWS, MID_L)
    none = jnp.zeros((1, ROWS, MID_L), BF)
    planes = [g1[:wide], None, None, g1[wide : 2 * wide]]
    for x in (1, 2):
        other = g1[2 * wide + x - 1 : 2 * wide + x]
        low = jnp.where(core == 1, other, none)
        high = jnp.where(core == 0, other, none)
        planes[x] = jnp.concatenate([low, t_ref[x - 1], high], axis=0)
    for x in range(4):
        o_ref[x, :, :, :MID_L] = planes[x]
        edge = edges(planes[x].reshape(-1, MID_L).astype(F32), 0, 128)
        o_ref[x, :, :, MID_L:] = edge.astype(BF).reshape(wide, ROWS, 128)


def input_grad_body(t_ref, r1_ref, o_ref):
    o_ref[...] = adjoint(t_ref, r1_ref, *o_ref.shape[:2]).astype(BF).reshape(o_ref.shape)


def finish_body(m_ref, h_ref, w2_ref, b2_ref, w1_ref, b1_ref, pack2, pack1):
    which = parity()
    first = lax.axis_index("dp") % 2
    for ref, of in ((m_ref, which), (h_ref, 1 - which)):
        for at, half in ((0, first), (32, 1 - first)):
            rows = pl.ds(half * 32 + of * 16, 16)
            pack2[rows, :PACK1] = ref[at : at + 16].astype(F32)
            pack2[rows, PACK1:] = ref[at + 16 : at + 32].astype(F32)
        pack1[pl.ds(of * 32, 32), :] = ref[64:].astype(F32)
    row = lax.broadcasted_iota(jnp.int32, (64, 64), 0)
    col = lax.broadcasted_iota(jnp.int32, (64, 64), 1)
    for pack, w_ref, b_ref in ((pack2, w2_ref, b2_ref), (pack1, w1_ref, b1_ref)):
        width = w_ref.shape[1]
        w_ref[...] = pack[:, :width]
        spot = jnp.broadcast_to(pack[:, width : width + 1], (64, 64))
        b_ref[...] = jnp.sum(jnp.where(row == col, spot, 0.0), axis=0, keepdims=True)


def swap(cells, axis, bit):
    return lax.ppermute(cells, axis, [(i, i ^ bit) for i in range(lax.axis_size(axis))])


def pair_swap(cells, first):
    count = lax.axis_size("space")
    pairs = [(i, i + 1) for i in range(first, count - 1, 2)]
    return lax.ppermute(cells, "space", pairs + [(j, i) for i, j in pairs])


def halo(own, edge, *ready):
    side, *ready = hold((swap(edge, "ysp", 1), *ready))
    cells = jnp.concatenate([own, side], axis=1)
    even = pair_swap(cells, 0)
    odd = pair_swap(cells, 1)
    return side, even, odd, *ready


def powers(axis, first):
    return [m for m in (1, 2, 4, 8, 16, 32, 64) if first <= m < lax.axis_size(axis)]


def cross(cells, axis, bit):
    pairs = [(2 * i + c, 2 * (i ^ bit) + 1 - c) for i in range(lax.axis_size(axis)) for c in range(2)]
    return lax.ppermute(cells, (axis, "ysp"), pairs)


def on_device(inputs, w_first, b_first, w_second, b_second, cotangent):
    nx, ny = inputs.shape[1], inputs.shape[2]
    own = inputs.reshape(nx, ny, ROWS, IN_L)
    edge = lax.dynamic_slice_in_dim(own, (1 - lax.axis_index("ysp")) * (ny - 2), 2, axis=1)
    side, even, odd = halo(own, edge)
    hbm = pl.BlockSpec(memory_space=pltpu.HBM)
    banded = call(
        banded_body,
        2000000000,
        [
            ((256, 9 * 256), BF),
            ((256, 9 * 384), BF),
            ((9, 384, 256), BF),
            ((9, 384, 128), BF),
            ((2, MID_L), F32),
        ],
        [
            pltpu.VMEM((64, W1_L), F32),
            pltpu.VMEM((64, W2_L), F32),
            pltpu.VMEM((2, C_MID), F32),
            pltpu.SemaphoreType.DMA((4,)),
        ],
        vmem=16 << 20,
        in_specs=[hbm] * 4,
    )(*[pltpu.with_memory_space_constraint(v, pltpu.HBM) for v in (w_first.T, w_second.T, b_first.reshape(1, C_MID), b_second.reshape(1, C_MID))])
    cot = cotangent.reshape(nx, ny, ROWS, MID_L)
    odd, even, cot, f1, f2, r2, r1, bias = hold((odd, even, cot, *banded))
    wide_in, act, y1, out, g2, edge = call(
        forward_body,
        4800000000,
        [
            ((nx + 4, ny + 4, ROWS, 256), BF),
            ((nx + 2, ny + 2, ROWS, 384), BF),
            ((nx + 2, ny + 2, ROWS, MID_L), F32),
            ((nx, ny, ROWS, MID_L), BF),
            ((nx, ny, ROWS, MID_L), BF),
            ((nx, 2, ROWS, MID_L), BF),
        ],
        [pltpu.VMEM(((nx + 2) * (ny + 2) * ROWS, MID_L), F32)],
    )(own, side, even, odd, f1, f2, bias, cot)
    keep2, send2, slope = call(
        second_weights_body,
        1800000000,
        [((32, PACK2), F32), ((32, PACK2), BF), ((nx + 2, ny + 2, ROWS, MID_L), F32)],
        [pltpu.VMEM((64, PACK2), F32)],
    )(act, g2, y1)
    side, even, odd, keep2, send2, slope = halo(g2, edge, keep2, send2, slope)
    got2 = cross(send2, "dp", 1)
    odd, even, keep2, got2 = hold((odd, even, keep2, got2))
    keep, send, g1 = call(
        backward_body,
        5600000000,
        [((64, PACK1), F32), ((64, PACK1), BF), ((nx, ny, ROWS, MID_L), BF)],
        [
            pltpu.VMEM((nx + 2, ny + 2, ROWS, 384), BF),
            pltpu.VMEM((64, PACK1), F32),
            pltpu.VMEM((32, PACK2), F32),
        ],
    )(g2, side, even, odd, r2, slope, wide_in, keep2, got2)
    total = hold((keep + swap(send, "ysp", 1).astype(F32)).astype(BF))
    sum1, sum2 = hold((total[:32], total[32:]))
    (wide_g,) = call(
        outer_body,
        1400000000,
        [((nx + 2, ny + 2, ROWS, 384), BF)],
        [pltpu.VMEM((nx + 4, ny + 4, ROWS, 384), BF)],
    )(g2, side, even, odd, r2, slope, g1)
    output = out.reshape(1, nx, ny, DEPTH * C_MID)
    along = [("space", m) for m in powers("space", 1)]
    stages1 = [("dp", m) for m in powers("dp", 1)] + along
    stages2 = [("dp", m) for m in powers("dp", 2)] + along
    for at, (one, two) in enumerate(zip(stages1, [*stages2, None])):
        got1 = cross(sum1, *one)
        got2 = cross(sum2, *(two or ("dp", 1)))
        if at == 0:
            got1, wide_g = hold((got1, wide_g))
            (d_in,) = call(input_grad_body, 1200000000, [((nx, ny, ROWS, IN_L), BF)])(wide_g, r1)
            input_grad = d_in.reshape(1, nx, ny, DEPTH * C_IN)
        if at == 2:
            got1, output = hold((got1, output))
        if at == 2:
            got1, input_grad = hold((got1, input_grad))
        sum1 = hold(sum1 + got1)
        if two:
            sum2 = hold(sum2 + got2)
    total = jnp.concatenate([sum2, got2, sum1], axis=0)
    gw2, gb2, gw1, gb1 = call(
        finish_body,
        1200000000,
        [((64, W2_L), F32), ((1, 64), F32), ((64, W1_L), F32), ((1, 64), F32)],
        [pltpu.VMEM((64, PACK2), F32), pltpu.VMEM((64, PACK1), F32)],
    )(total, swap(total, "ysp", 1))
    return (output, input_grad, gw1.T, gb1.reshape(64), gw2.T, gb2.reshape(64))


def solution(mesh):
    placed = P(("groups", "dp"), "space", "ysp", None)
    return jax.shard_map(
        on_device,
        mesh=mesh,
        in_specs=(placed, P(), P(), P(), P(), placed),
        out_specs=(placed, placed, P("groups", None), P("groups"), P("groups", None), P("groups")),
        check_vma=False,
    )
```

```python
import jax
import jax.numpy as jnp
from jax import lax
from jax.experimental import pallas as pl
from jax.experimental.pallas import tpu as pltpu
from jax.sharding import PartitionSpec as P

C_IN = 32
C_MID = 64
DEPTH = 64
BF = jnp.bfloat16
F32 = jnp.float32
hold = lax.optimization_barrier
GROUP = 4
ROWS = DEPTH // GROUP
IN_L = GROUP * C_IN
MID_L = GROUP * C_MID
TAP1 = 3 * C_IN
TAP2 = 3 * C_MID
W1_L = 9 * TAP1
W2_L = 9 * TAP2
PACK2 = 1792
PACK1 = 896
NT = (((1,), (1,)), ((), ()))
NN = (((1,), (0,)), ((), ()))


def call(body, flops, outs, scratch=(), vmem=16 << 20, **specs):
    return pl.pallas_call(
        body,
        out_shape=[jax.ShapeDtypeStruct(shape, kind) for shape, kind in outs],
        scratch_shapes=list(scratch),
        compiler_params=pltpu.CompilerParams(vmem_limit_bytes=vmem),
        cost_estimate=pl.CostEstimate(flops=flops, bytes_accessed=flops // 256, transcendentals=0),
        **specs,
    )


def dot(a, b, dims):
    return lax.dot_general(a, b, dims, preferred_element_type=F32)


def window(ref, start, width):
    frame = 256 if width <= 128 else 384
    at = start // 128 * 128
    stop = min(at + frame, ref.shape[1])
    value = ref[:, at:stop]
    if stop < at + frame:
        value = jnp.concatenate([value, jnp.zeros((64, at + frame - stop), F32)], axis=1)
    if start != at:
        value = pltpu.roll(value, frame - (start - at), 1)
    lane = lax.broadcasted_iota(jnp.int32, value.shape, 1)
    return jnp.where(lane < width, value, 0.0)


def banded_body(w1_ref, w2_ref, b1_ref, b2_ref, f1_ref, f2_ref, r2_ref, r1_ref, bias_ref, pad1, pad2, lines, sems):
    copies = [
        pltpu.make_async_copy(w1_ref, pad1, sems.at[0]),
        pltpu.make_async_copy(w2_ref, pad2, sems.at[1]),
        pltpu.make_async_copy(b1_ref, lines.at[pl.ds(0, 1)], sems.at[2]),
        pltpu.make_async_copy(b2_ref, lines.at[pl.ds(1, 1)], sems.at[3]),
    ]
    for copy in copies:
        copy.start()
    for copy in copies:
        copy.wait()
    bias_ref[...] = jnp.concatenate([lines[...]] * GROUP, axis=1)
    for tap in range(9):
        one = window(pad1, tap * TAP1, TAP1)
        two = window(pad2, tap * TAP2, TAP2)
        for m in range(-1, 5):
            at = (m % 6) * C_MID
            s1 = pltpu.roll(one, ((m - 1) * C_IN) % 256, 1) if m != 1 else one
            s2 = pltpu.roll(two, ((m - 1) * C_MID) % 384, 1) if m != 1 else two
            s1 = s1.astype(BF)
            s2 = s2.astype(BF)
            if 0 <= m < 4:
                f1_ref[m * C_MID : (m + 1) * C_MID, tap * 256 : (tap + 1) * 256] = s1
                f2_ref[m * C_MID : (m + 1) * C_MID, tap * 384 : (tap + 1) * 384] = s2
            r1_ref[tap, at : at + C_MID, :] = s1[:, :IN_L]
            r2_ref[tap, at : at + C_MID, :] = s2[:, :MID_L]


def edges(value, low, high):
    count = value.shape[0]
    row = lax.broadcasted_iota(jnp.int32, (count, 128), 0) % ROWS
    lane = lax.broadcasted_iota(jnp.int32, (count, 128), 1)
    after = pltpu.roll(value[:, low : low + 128], count - 1, 0)
    before = pltpu.roll(value[:, high : high + 128], 1, 0)
    after = jnp.where(row == ROWS - 1, 0.0, after)
    before = jnp.where(row == 0, 0.0, before)
    return jnp.where(lane < 64, after, before)


def spread(parts, core, to_ref, lanes):
    for x, (middle, side) in enumerate(parts):
        side = side.astype(F32)
        low = jnp.where(core == 1, side, 0.0)
        high = jnp.where(core == 0, side, 0.0)
        cells = jnp.concatenate([low, middle.astype(F32), high], axis=0)
        rows = cells.reshape(-1, lanes)
        shape = cells.shape[:2]
        to_ref[x, :, :, :lanes] = cells.astype(BF)
        edge = edges(rows, 0, lanes - 128)
        to_ref[x, :, :, lanes:] = edge.astype(BF).reshape(*shape, 128)


def gathered(own, side, even, odd, space):
    count, narrow = own.shape[:2]
    both = [(even[i], odd[i]) for i in range(even.shape[0])]
    flip = space % 2 == 1
    left = [jnp.where(flip, one, two) for one, two in both]
    right = [jnp.where(flip, two, one) for one, two in both]
    mid = [(own[i], side[i]) for i in range(count)]
    return [(p[:narrow], p[narrow:]) for p in left] + mid + [(p[:narrow], p[narrow:]) for p in right]


def taps(of):
    parts = [of(*divmod(tap, 3)) for tap in range(9)]
    return jnp.concatenate([part.reshape(-1, part.shape[-1]) for part in parts], axis=1)


def sigmoid(value):
    return 0.5 * jnp.tanh(0.5 * value) + 0.5


def plane_mask(x, rows, space, last, core):
    row = lax.broadcasted_iota(jnp.int32, (rows, 1), 0)
    inside = jnp.float32(1.0)
    if x == 0:
        inside = jnp.where(space > 0, 1.0, 0.0)
    if x == 3:
        inside = jnp.where(space < last, 1.0, 0.0)
    low = jnp.where(core == 1, 1.0, 0.0)
    high = jnp.where(core == 0, 1.0, 0.0)
    mask = jnp.where(row < ROWS, low, jnp.where(row >= rows - ROWS, high, 1.0))
    return mask * inside


def forward_body(x_ref, by_ref, ev_ref, od_ref, f1_ref, f2_ref, b_ref, c_ref, e_ref, a_ref, d_ref, o_ref, g_ref, n_ref, acc):
    core = lax.axis_index("ysp")
    space = lax.axis_index("space")
    last = lax.axis_size("space") - 1
    spread(gathered(x_ref, by_ref, ev_ref, od_ref, space), core, e_ref, IN_L)
    wide = x_ref.shape[1] + 2
    narrow = wide - 2
    acc[...] = dot(taps(lambda a, b: e_ref[a : a + 4, b : b + wide]), f1_ref[...], NT)
    rows = wide * ROWS
    bias1, bias2 = b_ref[0:1], b_ref[1:2]
    for x in range(4):
        y1 = acc[x * rows : (x + 1) * rows, :] + bias1
        mask = plane_mask(x, rows, space, last, core)
        sig = sigmoid(y1)
        d_ref[x] = y1.reshape(wide, ROWS, MID_L)
        act = (y1 * sig * mask).astype(BF)
        a_ref[x, :, :, :MID_L] = act.reshape(wide, ROWS, MID_L)
        edge = edges(act.astype(F32), 0, 128)
        a_ref[x, :, :, MID_L:] = edge.astype(BF).reshape(wide, ROWS, 128)
    y2 = dot(taps(lambda a, b: a_ref[a : a + 2, b : b + narrow]), f2_ref[...], NT) + bias2
    sig = sigmoid(y2)
    shape = o_ref.shape
    o_ref[...] = (y2 * sig).astype(BF).reshape(shape)
    cot = c_ref[...].reshape(-1, MID_L).astype(F32)
    g_ref[...] = (cot * (sig * (1.0 + y2 * (1.0 - sig)))).astype(BF).reshape(shape)
    n_ref[...] = g_ref[:, pl.ds((1 - core) * (narrow - 2), 2)]


def flipped(grads):
    turned = grads.astype(F32).T
    sums = jnp.sum(turned, axis=1, keepdims=True)
    bias = sums[0:64] + sums[64:128] + sums[128:192] + sums[192:256]
    return turned.astype(BF), bias


def tap_sum(product, step):
    frame = product.shape[1]
    total = product[64:128]
    for j in (0, 2, 3):
        total = total + pltpu.roll(product[j * 64 : (j + 1) * 64], (frame - (j - 1) * step) % frame, 1)
    return total


def second_weights_body(a_ref, g_ref, k_ref, s_ref, p_ref):
    turned, bias = flipped(g_ref[...].reshape(-1, MID_L))
    narrow = g_ref.shape[1]
    lane = lax.broadcasted_iota(jnp.int32, (64, 384), 1)
    held = None
    for tap in range(9):
        a, b = divmod(tap, 3)
        found = tap_sum(dot(turned, a_ref[a : a + 2, b : b + narrow].reshape(-1, 384), NN), C_MID)
        if tap == 8:
            p_ref[:, 1536:1792] = jnp.where(lane < TAP2, found, bias)[:, :256]
        elif tap % 2 == 0:
            held = found
        else:
            at = (tap - 1) * TAP2
            p_ref[:, at : at + 384] = jnp.where(lane < TAP2, held, pltpu.roll(found, TAP2, 1))
    k_ref[...], s_ref[...] = halves(p_ref, lax.axis_index("dp") % 2)


def slope_body(y_ref, d_ref):
    core = lax.axis_index("ysp")
    space = lax.axis_index("space")
    last = lax.axis_size("space") - 1
    rows = y_ref.shape[1] * ROWS
    for x in range(4):
        y1 = y_ref[x].reshape(rows, MID_L)
        sig = sigmoid(y1)
        slope = sig * (1.0 + y1 * (1.0 - sig)) * plane_mask(x, rows, space, last, core)
        d_ref[x] = slope.reshape(y_ref.shape[1:])


def parity():
    bits = lax.axis_index("ysp")
    for axis in ("dp", "space"):
        at, count = lax.axis_index(axis), lax.axis_size(axis)
        while count > 1:
            bits, at, count = bits + at % 2, at // 2, (count + 1) // 2
    return bits % 2


def halves(pack, which):
    count = pack.shape[0] // 2
    return pack[pl.ds(which * count, count), :], pack[pl.ds((1 - which) * count, count), :].astype(BF)


def adjoint(wide_ref, taps_ref, tall, wide):
    cells = taps(lambda a, b: wide_ref[2 - a : 2 - a + tall, 2 - b : 2 - b + wide])
    return dot(cells, taps_ref[...].reshape(9 * 384, -1), NN)


def backward_body(g_ref, by_ref, ev_ref, od_ref, r2_ref, d_ref, e_ref, k2_ref, h2_ref, k_ref, s_ref, t_ref, wide_g, pack, pack2):
    core = lax.axis_index("ysp")
    space = lax.axis_index("space")
    near = gathered(g_ref, by_ref, ev_ref, od_ref, space)[1:5]
    spread([(middle, jnp.where(core == 0, side[:1], side[1:])) for middle, side in near], core, wide_g, MID_L)
    narrow = g_ref.shape[1]
    slope = d_ref[1:3, 1 : 1 + narrow].reshape(-1, MID_L)
    g1 = (adjoint(wide_g, r2_ref, 2, narrow) * slope).astype(BF)
    t_ref[...] = g1.reshape(t_ref.shape)
    turned, bias = flipped(g1)
    lane = lax.broadcasted_iota(jnp.int32, (64, 384), 1)
    none = jnp.zeros((64, 128), F32)
    held = None
    for tap in range(9):
        a, b = divmod(tap, 3)
        cells = e_ref[1 + a : 3 + a, 1 + b : 1 + b + narrow].reshape(-1, 256)
        found = tap_sum(dot(turned, cells, NN), C_IN)
        if tap == 8:
            pack[:, 768:896] = jnp.where(lane < TAP1, jnp.concatenate([found, none], axis=1), bias)[:, :128]
            continue
        found = jnp.concatenate([found, none], axis=1)
        slot = tap % 4
        if slot == 0:
            held = found
        else:
            held = jnp.where(lane < slot * TAP1, held, pltpu.roll(found, slot * TAP1, 1))
        if slot == 3:
            at = (tap - 3) * TAP1
            pack[:, at : at + 384] = held
    which = parity()
    k_ref[:32], s_ref[:32] = halves(pack, which)
    pack2[...] = k2_ref[...] + h2_ref[...].astype(F32)
    keep, send = halves(pack2, which)
    k_ref[32:48], k_ref[48:] = keep[:, :PACK1], keep[:, PACK1:]
    s_ref[32:48], s_ref[48:] = send[:, :PACK1], send[:, PACK1:]


def outer_body(g_ref, by_ref, ev_ref, od_ref, r2_ref, d_ref, t_ref, o_ref, wide_g):
    core = lax.axis_index("ysp")
    space = lax.axis_index("space")
    spread(gathered(g_ref, by_ref, ev_ref, od_ref, space), core, wide_g, MID_L)
    narrow = g_ref.shape[1]
    wide = narrow + 2
    at = (1 - core) * (wide - 1)

    def around(a, b):
        cols = pl.ds(2 - b, wide)
        beside = wide_g[3 - a : 5 - a, pl.ds(2 - b + at, 1)]
        return jnp.concatenate([wide_g[2 - a, cols], wide_g[5 - a, cols], beside[:, 0]], axis=0)

    slope = jnp.concatenate([d_ref[0], d_ref[3], d_ref[1:3, pl.ds(at, 1)][:, 0]], axis=0)
    g1 = dot(taps(around), r2_ref[...].reshape(9 * 384, -1), NN) * slope.reshape(-1, MID_L)
    g1 = g1.astype(BF).reshape(-1, ROWS, MID_L)
    none = jnp.zeros((1, ROWS, MID_L), BF)
    planes = [g1[:wide], None, None, g1[wide : 2 * wide]]
    for x in (1, 2):
        other = g1[2 * wide + x - 1 : 2 * wide + x]
        low = jnp.where(core == 1, other, none)
        high = jnp.where(core == 0, other, none)
        planes[x] = jnp.concatenate([low, t_ref[x - 1], high], axis=0)
    for x in range(4):
        o_ref[x, :, :, :MID_L] = planes[x]
        edge = edges(planes[x].reshape(-1, MID_L).astype(F32), 0, 128)
        o_ref[x, :, :, MID_L:] = edge.astype(BF).reshape(wide, ROWS, 128)


def input_grad_body(t_ref, r1_ref, o_ref):
    o_ref[...] = adjoint(t_ref, r1_ref, *o_ref.shape[:2]).astype(BF).reshape(o_ref.shape)


def finish_body(m_ref, h_ref, w2_ref, b2_ref, w1_ref, b1_ref, pack2, pack1):
    which = parity()
    first = lax.axis_index("dp") % 2
    for ref, of in ((m_ref, which), (h_ref, 1 - which)):
        for at, half in ((0, first), (32, 1 - first)):
            rows = pl.ds(half * 32 + of * 16, 16)
            pack2[rows, :PACK1] = ref[at : at + 16].astype(F32)
            pack2[rows, PACK1:] = ref[at + 16 : at + 32].astype(F32)
        pack1[pl.ds(of * 32, 32), :] = ref[64:].astype(F32)
    row = lax.broadcasted_iota(jnp.int32, (64, 64), 0)
    col = lax.broadcasted_iota(jnp.int32, (64, 64), 1)
    for pack, w_ref, b_ref in ((pack2, w2_ref, b2_ref), (pack1, w1_ref, b1_ref)):
        width = w_ref.shape[1]
        w_ref[...] = pack[:, :width]
        spot = jnp.broadcast_to(pack[:, width : width + 1], (64, 64))
        b_ref[...] = jnp.sum(jnp.where(row == col, spot, 0.0), axis=0, keepdims=True)


def swap(cells, axis, bit):
    return lax.ppermute(cells, axis, [(i, i ^ bit) for i in range(lax.axis_size(axis))])


def pair_swap(cells, first):
    count = lax.axis_size("space")
    pairs = [(i, i + 1) for i in range(first, count - 1, 2)]
    return lax.ppermute(cells, "space", pairs + [(j, i) for i, j in pairs])


def halo(own, edge, *ready):
    side, *ready = hold((swap(edge, "ysp", 1), *ready))
    cells = jnp.concatenate([own, side], axis=1)
    even = pair_swap(cells, 0)
    odd = pair_swap(cells, 1)
    return side, even, odd, *ready


def powers(axis, first):
    return [m for m in (1, 2, 4, 8, 16, 32, 64) if first <= m < lax.axis_size(axis)]


def cross(cells, axis, bit):
    pairs = [(2 * i + c, 2 * (i ^ bit) + 1 - c) for i in range(lax.axis_size(axis)) for c in range(2)]
    return lax.ppermute(cells, (axis, "ysp"), pairs)


def on_device(inputs, w_first, b_first, w_second, b_second, cotangent):
    nx, ny = inputs.shape[1], inputs.shape[2]
    own = inputs.reshape(nx, ny, ROWS, IN_L)
    edge = lax.dynamic_slice_in_dim(own, (1 - lax.axis_index("ysp")) * (ny - 2), 2, axis=1)
    side, even, odd = halo(own, edge)
    hbm = pl.BlockSpec(memory_space=pltpu.HBM)
    banded = call(
        banded_body,
        2000000000,
        [
            ((256, 9 * 256), BF),
            ((256, 9 * 384), BF),
            ((9, 384, 256), BF),
            ((9, 384, 128), BF),
            ((2, MID_L), F32),
        ],
        [
            pltpu.VMEM((64, W1_L), F32),
            pltpu.VMEM((64, W2_L), F32),
            pltpu.VMEM((2, C_MID), F32),
            pltpu.SemaphoreType.DMA((4,)),
        ],
        vmem=16 << 20,
        in_specs=[hbm] * 4,
    )(*[pltpu.with_memory_space_constraint(v, pltpu.HBM) for v in (w_first.T, w_second.T, b_first.reshape(1, C_MID), b_second.reshape(1, C_MID))])
    cot = cotangent.reshape(nx, ny, ROWS, MID_L)
    even, odd, cot, f1, f2, r2, r1, bias = hold((even, odd, cot, *banded))
    wide_in, act, y1, out, g2, edge = call(
        forward_body,
        4800000000,
        [
            ((nx + 4, ny + 4, ROWS, 256), BF),
            ((nx + 2, ny + 2, ROWS, 384), BF),
            ((nx + 2, ny + 2, ROWS, MID_L), F32),
            ((nx, ny, ROWS, MID_L), BF),
            ((nx, ny, ROWS, MID_L), BF),
            ((nx, 2, ROWS, MID_L), BF),
        ],
        [pltpu.VMEM(((nx + 2) * (ny + 2) * ROWS, MID_L), F32)],
    )(own, side, even, odd, f1, f2, bias, cot)
    keep2, send2 = call(
        second_weights_body, 1800000000, [((32, PACK2), F32), ((32, PACK2), BF)], [pltpu.VMEM((64, PACK2), F32)]
    )(act, g2)
    side, even, odd, keep2, send2, y1 = halo(g2, edge, keep2, send2, y1)
    got2 = cross(send2, "dp", 1)
    (slope,) = call(slope_body, 1600000000, [((nx + 2, ny + 2, ROWS, MID_L), F32)])(y1)
    odd, even, keep2, got2, slope = hold((odd, even, keep2, got2, slope))
    keep, send, g1 = call(
        backward_body,
        5600000000,
        [((64, PACK1), F32), ((64, PACK1), BF), ((nx, ny, ROWS, MID_L), BF)],
        [
            pltpu.VMEM((nx + 2, ny + 2, ROWS, 384), BF),
            pltpu.VMEM((64, PACK1), F32),
            pltpu.VMEM((32, PACK2), F32),
        ],
    )(g2, side, even, odd, r2, slope, wide_in, keep2, got2)
    total = hold((keep + swap(send, "ysp", 1).astype(F32)).astype(BF))
    sum1, sum2 = hold((total[:32], total[32:]))
    (wide_g,) = call(
        outer_body,
        1400000000,
        [((nx + 2, ny + 2, ROWS, 384), BF)],
        [pltpu.VMEM((nx + 4, ny + 4, ROWS, 384), BF)],
    )(g2, side, even, odd, r2, slope, g1)
    output = out.reshape(1, nx, ny, DEPTH * C_MID)
    along = [("space", m) for m in powers("space", 1)]
    stages1 = [("dp", m) for m in powers("dp", 1)] + along
    stages2 = [("dp", m) for m in powers("dp", 2)] + along
    for at, (one, two) in enumerate(zip(stages1, [*stages2, None])):
        got1 = cross(sum1, *one)
        got2 = cross(sum2, *(two or ("dp", 1)))
        if at == 0:
            got1, wide_g = hold((got1, wide_g))
            (d_in,) = call(input_grad_body, 1200000000, [((nx, ny, ROWS, IN_L), BF)])(wide_g, r1)
            input_grad = d_in.reshape(1, nx, ny, DEPTH * C_IN)
        if at == 2:
            got1, output = hold((got1, output))
        if at == 2:
            got1, input_grad = hold((got1, input_grad))
        sum1 = hold(sum1 + got1)
        if two:
            sum2 = hold(sum2 + got2)
    total = jnp.concatenate([sum2, got2, sum1], axis=0)
    gw2, gb2, gw1, gb1 = call(
        finish_body,
        1200000000,
        [((64, W2_L), F32), ((1, 64), F32), ((64, W1_L), F32), ((1, 64), F32)],
        [pltpu.VMEM((64, PACK2), F32), pltpu.VMEM((64, PACK1), F32)],
    )(total, swap(total, "ysp", 1))
    return (output, input_grad, gw1.T, gb1.reshape(64), gw2.T, gb2.reshape(64))


def solution(mesh):
    placed = P(("groups", "dp"), "space", "ysp", None)
    return jax.shard_map(
        on_device,
        mesh=mesh,
        in_specs=(placed, P(), P(), P(), P(), placed),
        out_specs=(placed, placed, P("groups", None), P("groups"), P("groups", None), P("groups")),
        check_vma=False,
    )
```

```python
import jax
import jax.numpy as jnp
from jax import lax
from jax.experimental import pallas as pl
from jax.experimental.pallas import tpu as pltpu
from jax.sharding import PartitionSpec as P

C_IN = 32
C_MID = 64
DEPTH = 64
BF = jnp.bfloat16
F32 = jnp.float32
hold = lax.optimization_barrier
GROUP = 4
ROWS = DEPTH // GROUP
IN_L = GROUP * C_IN
MID_L = GROUP * C_MID
TAP1 = 3 * C_IN
TAP2 = 3 * C_MID
W1_L = 9 * TAP1
W2_L = 9 * TAP2
PACK2 = 1792
PACK1 = 896
NT = (((1,), (1,)), ((), ()))
NN = (((1,), (0,)), ((), ()))


def call(body, flops, outs, scratch=(), vmem=16 << 20, **specs):
    return pl.pallas_call(
        body,
        out_shape=[jax.ShapeDtypeStruct(shape, kind) for shape, kind in outs],
        scratch_shapes=list(scratch),
        compiler_params=pltpu.CompilerParams(vmem_limit_bytes=vmem),
        cost_estimate=pl.CostEstimate(flops=flops, bytes_accessed=flops // 256, transcendentals=0),
        **specs,
    )


def dot(a, b, dims):
    return lax.dot_general(a, b, dims, preferred_element_type=F32)


def window(ref, start, width):
    frame = 256 if width <= 128 else 384
    at = start // 128 * 128
    stop = min(at + frame, ref.shape[1])
    value = ref[:, at:stop]
    if stop < at + frame:
        value = jnp.concatenate([value, jnp.zeros((64, at + frame - stop), F32)], axis=1)
    if start != at:
        value = pltpu.roll(value, frame - (start - at), 1)
    lane = lax.broadcasted_iota(jnp.int32, value.shape, 1)
    return jnp.where(lane < width, value, 0.0)


def banded_body(w1_ref, w2_ref, b1_ref, b2_ref, f1_ref, f2_ref, r2_ref, r1_ref, bias_ref, pad1, pad2, lines, sems):
    copies = [
        pltpu.make_async_copy(w1_ref, pad1, sems.at[0]),
        pltpu.make_async_copy(w2_ref, pad2, sems.at[1]),
        pltpu.make_async_copy(b1_ref, lines.at[pl.ds(0, 1)], sems.at[2]),
        pltpu.make_async_copy(b2_ref, lines.at[pl.ds(1, 1)], sems.at[3]),
    ]
    for copy in copies:
        copy.start()
    for copy in copies:
        copy.wait()
    bias_ref[...] = jnp.concatenate([lines[...]] * GROUP, axis=1)
    for tap in range(9):
        one = window(pad1, tap * TAP1, TAP1)
        two = window(pad2, tap * TAP2, TAP2)
        for m in range(-1, 5):
            at = (m % 6) * C_MID
            s1 = pltpu.roll(one, ((m - 1) * C_IN) % 256, 1) if m != 1 else one
            s2 = pltpu.roll(two, ((m - 1) * C_MID) % 384, 1) if m != 1 else two
            s1 = s1.astype(BF)
            s2 = s2.astype(BF)
            if 0 <= m < 4:
                f1_ref[m * C_MID : (m + 1) * C_MID, tap * 256 : (tap + 1) * 256] = s1
                f2_ref[m * C_MID : (m + 1) * C_MID, tap * 384 : (tap + 1) * 384] = s2
            r1_ref[tap, at : at + C_MID, :] = s1[:, :IN_L]
            r2_ref[tap, at : at + C_MID, :] = s2[:, :MID_L]


def edges(value, low, high):
    count = value.shape[0]
    row = lax.broadcasted_iota(jnp.int32, (count, 128), 0) % ROWS
    lane = lax.broadcasted_iota(jnp.int32, (count, 128), 1)
    after = pltpu.roll(value[:, low : low + 128], count - 1, 0)
    before = pltpu.roll(value[:, high : high + 128], 1, 0)
    after = jnp.where(row == ROWS - 1, 0.0, after)
    before = jnp.where(row == 0, 0.0, before)
    return jnp.where(lane < 64, after, before)


def spread(parts, core, to_ref, lanes):
    for x, (middle, side) in enumerate(parts):
        side = side.astype(F32)
        low = jnp.where(core == 1, side, 0.0)
        high = jnp.where(core == 0, side, 0.0)
        cells = jnp.concatenate([low, middle.astype(F32), high], axis=0)
        rows = cells.reshape(-1, lanes)
        shape = cells.shape[:2]
        to_ref[x, :, :, :lanes] = cells.astype(BF)
        edge = edges(rows, 0, lanes - 128)
        to_ref[x, :, :, lanes:] = edge.astype(BF).reshape(*shape, 128)


def gathered(own, side, even, odd, space):
    count, narrow = own.shape[:2]
    both = [(even[i], odd[i]) for i in range(even.shape[0])]
    flip = space % 2 == 1
    left = [jnp.where(flip, one, two) for one, two in both]
    right = [jnp.where(flip, two, one) for one, two in both]
    mid = [(own[i], side[i]) for i in range(count)]
    return [(p[:narrow], p[narrow:]) for p in left] + mid + [(p[:narrow], p[narrow:]) for p in right]


def taps(of):
    parts = [of(*divmod(tap, 3)) for tap in range(9)]
    return jnp.concatenate([part.reshape(-1, part.shape[-1]) for part in parts], axis=1)


def sigmoid(value):
    return 0.5 * jnp.tanh(0.5 * value) + 0.5


def plane_mask(x, rows, space, last, core):
    row = lax.broadcasted_iota(jnp.int32, (rows, 1), 0)
    inside = jnp.float32(1.0)
    if x == 0:
        inside = jnp.where(space > 0, 1.0, 0.0)
    if x == 3:
        inside = jnp.where(space < last, 1.0, 0.0)
    low = jnp.where(core == 1, 1.0, 0.0)
    high = jnp.where(core == 0, 1.0, 0.0)
    mask = jnp.where(row < ROWS, low, jnp.where(row >= rows - ROWS, high, 1.0))
    return mask * inside


def forward_body(x_ref, by_ref, ev_ref, od_ref, f1_ref, f2_ref, b_ref, c_ref, e_ref, a_ref, d_ref, o_ref, g_ref, n_ref, acc):
    core = lax.axis_index("ysp")
    space = lax.axis_index("space")
    last = lax.axis_size("space") - 1
    spread(gathered(x_ref, by_ref, ev_ref, od_ref, space), core, e_ref, IN_L)
    wide = x_ref.shape[1] + 2
    narrow = wide - 2
    at, most = 1 - core, wide - 1
    acc[...] = dot(taps(lambda a, b: e_ref[a : a + 4, pl.ds(b + at, most)]), f1_ref[...], NT)
    rows = most * ROWS
    bias1, bias2 = b_ref[0:1], b_ref[1:2]
    for x in range(4):
        y1 = acc[x * rows : (x + 1) * rows, :] + bias1
        act = y1 * sigmoid(y1)
        if x in (0, 3):
            act = act * jnp.where((space > 0) if x == 0 else (space < last), 1.0, 0.0)
        act = act.astype(BF)
        d_ref[x, pl.ds(at, most)] = y1.reshape(most, ROWS, MID_L)
        d_ref[x, core * most] = jnp.zeros((ROWS, MID_L), F32)
        a_ref[x, pl.ds(at, most), :, :MID_L] = act.reshape(most, ROWS, MID_L)
        edge = edges(act.astype(F32), 0, 128)
        a_ref[x, pl.ds(at, most), :, MID_L:] = edge.astype(BF).reshape(most, ROWS, 128)
        a_ref[x, core * most] = jnp.zeros((ROWS, 384), BF)
    y2 = dot(taps(lambda a, b: a_ref[a : a + 2, b : b + narrow]), f2_ref[...], NT) + bias2
    sig = sigmoid(y2)
    shape = o_ref.shape
    o_ref[...] = (y2 * sig).astype(BF).reshape(shape)
    cot = c_ref[...].reshape(-1, MID_L).astype(F32)
    g_ref[...] = (cot * (sig * (1.0 + y2 * (1.0 - sig)))).astype(BF).reshape(shape)
    n_ref[...] = g_ref[:, pl.ds((1 - core) * (narrow - 2), 2)]


def flipped(grads):
    turned = grads.astype(F32).T
    sums = jnp.sum(turned, axis=1, keepdims=True)
    bias = sums[0:64] + sums[64:128] + sums[128:192] + sums[192:256]
    return turned.astype(BF), bias


def tap_sum(product, step):
    frame = product.shape[1]
    total = product[64:128]
    for j in (0, 2, 3):
        total = total + pltpu.roll(product[j * 64 : (j + 1) * 64], (frame - (j - 1) * step) % frame, 1)
    return total


def second_weights_body(a_ref, g_ref, k_ref, s_ref, p_ref):
    turned, bias = flipped(g_ref[...].reshape(-1, MID_L))
    narrow = g_ref.shape[1]
    lane = lax.broadcasted_iota(jnp.int32, (64, 384), 1)
    held = None
    for tap in range(9):
        a, b = divmod(tap, 3)
        found = tap_sum(dot(turned, a_ref[a : a + 2, b : b + narrow].reshape(-1, 384), NN), C_MID)
        if tap == 8:
            p_ref[:, 1536:1792] = jnp.where(lane < TAP2, found, bias)[:, :256]
        elif tap % 2 == 0:
            held = found
        else:
            at = (tap - 1) * TAP2
            p_ref[:, at : at + 384] = jnp.where(lane < TAP2, held, pltpu.roll(found, TAP2, 1))
    k_ref[...], s_ref[...] = halves(p_ref, lax.axis_index("dp") % 2)


def slope_body(y_ref, d_ref):
    core = lax.axis_index("ysp")
    space = lax.axis_index("space")
    last = lax.axis_size("space") - 1
    rows = y_ref.shape[1] * ROWS
    for x in range(4):
        y1 = y_ref[x].reshape(rows, MID_L)
        sig = sigmoid(y1)
        slope = sig * (1.0 + y1 * (1.0 - sig)) * plane_mask(x, rows, space, last, core)
        d_ref[x] = slope.reshape(y_ref.shape[1:])


def parity():
    bits = lax.axis_index("ysp")
    for axis in ("dp", "space"):
        at, count = lax.axis_index(axis), lax.axis_size(axis)
        while count > 1:
            bits, at, count = bits + at % 2, at // 2, (count + 1) // 2
    return bits % 2


def halves(pack, which):
    count = pack.shape[0] // 2
    return pack[pl.ds(which * count, count), :], pack[pl.ds((1 - which) * count, count), :].astype(BF)


def adjoint(wide_ref, taps_ref, tall, wide):
    cells = taps(lambda a, b: wide_ref[2 - a : 2 - a + tall, 2 - b : 2 - b + wide])
    return dot(cells, taps_ref[...].reshape(9 * 384, -1), NN)


def backward_body(g_ref, by_ref, ev_ref, od_ref, r2_ref, d_ref, e_ref, k2_ref, h2_ref, k_ref, s_ref, t_ref, wide_g, pack, pack2):
    core = lax.axis_index("ysp")
    space = lax.axis_index("space")
    near = gathered(g_ref, by_ref, ev_ref, od_ref, space)[1:5]
    spread([(middle, jnp.where(core == 0, side[:1], side[1:])) for middle, side in near], core, wide_g, MID_L)
    narrow = g_ref.shape[1]
    slope = d_ref[1:3, 1 : 1 + narrow].reshape(-1, MID_L)
    g1 = (adjoint(wide_g, r2_ref, 2, narrow) * slope).astype(BF)
    t_ref[...] = g1.reshape(t_ref.shape)
    turned, bias = flipped(g1)
    lane = lax.broadcasted_iota(jnp.int32, (64, 384), 1)
    none = jnp.zeros((64, 128), F32)
    held = None
    for tap in range(9):
        a, b = divmod(tap, 3)
        cells = e_ref[1 + a : 3 + a, 1 + b : 1 + b + narrow].reshape(-1, 256)
        found = tap_sum(dot(turned, cells, NN), C_IN)
        if tap == 8:
            pack[:, 768:896] = jnp.where(lane < TAP1, jnp.concatenate([found, none], axis=1), bias)[:, :128]
            continue
        found = jnp.concatenate([found, none], axis=1)
        slot = tap % 4
        if slot == 0:
            held = found
        else:
            held = jnp.where(lane < slot * TAP1, held, pltpu.roll(found, slot * TAP1, 1))
        if slot == 3:
            at = (tap - 3) * TAP1
            pack[:, at : at + 384] = held
    which = parity()
    k_ref[:32], s_ref[:32] = halves(pack, which)
    pack2[...] = k2_ref[...] + h2_ref[...].astype(F32)
    keep, send = halves(pack2, which)
    k_ref[32:48], k_ref[48:] = keep[:, :PACK1], keep[:, PACK1:]
    s_ref[32:48], s_ref[48:] = send[:, :PACK1], send[:, PACK1:]


def outer_body(g_ref, by_ref, ev_ref, od_ref, r2_ref, d_ref, t_ref, o_ref, wide_g):
    core = lax.axis_index("ysp")
    space = lax.axis_index("space")
    spread(gathered(g_ref, by_ref, ev_ref, od_ref, space), core, wide_g, MID_L)
    narrow = g_ref.shape[1]
    wide = narrow + 2
    at = (1 - core) * (wide - 1)

    def around(a, b):
        cols = pl.ds(2 - b, wide)
        beside = wide_g[3 - a : 5 - a, pl.ds(2 - b + at, 1)]
        return jnp.concatenate([wide_g[2 - a, cols], wide_g[5 - a, cols], beside[:, 0]], axis=0)

    slope = jnp.concatenate([d_ref[0], d_ref[3], d_ref[1:3, pl.ds(at, 1)][:, 0]], axis=0)
    g1 = dot(taps(around), r2_ref[...].reshape(9 * 384, -1), NN) * slope.reshape(-1, MID_L)
    g1 = g1.astype(BF).reshape(-1, ROWS, MID_L)
    none = jnp.zeros((1, ROWS, MID_L), BF)
    planes = [g1[:wide], None, None, g1[wide : 2 * wide]]
    for x in (1, 2):
        other = g1[2 * wide + x - 1 : 2 * wide + x]
        low = jnp.where(core == 1, other, none)
        high = jnp.where(core == 0, other, none)
        planes[x] = jnp.concatenate([low, t_ref[x - 1], high], axis=0)
    for x in range(4):
        o_ref[x, :, :, :MID_L] = planes[x]
        edge = edges(planes[x].reshape(-1, MID_L).astype(F32), 0, 128)
        o_ref[x, :, :, MID_L:] = edge.astype(BF).reshape(wide, ROWS, 128)


def input_grad_body(t_ref, r1_ref, o_ref):
    o_ref[...] = adjoint(t_ref, r1_ref, *o_ref.shape[:2]).astype(BF).reshape(o_ref.shape)


def finish_body(m_ref, h_ref, w2_ref, b2_ref, w1_ref, b1_ref, pack2, pack1):
    which = parity()
    first = lax.axis_index("dp") % 2
    for ref, of in ((m_ref, which), (h_ref, 1 - which)):
        for at, half in ((0, first), (32, 1 - first)):
            rows = pl.ds(half * 32 + of * 16, 16)
            pack2[rows, :PACK1] = ref[at : at + 16].astype(F32)
            pack2[rows, PACK1:] = ref[at + 16 : at + 32].astype(F32)
        pack1[pl.ds(of * 32, 32), :] = ref[64:].astype(F32)
    row = lax.broadcasted_iota(jnp.int32, (64, 64), 0)
    col = lax.broadcasted_iota(jnp.int32, (64, 64), 1)
    for pack, w_ref, b_ref in ((pack2, w2_ref, b2_ref), (pack1, w1_ref, b1_ref)):
        width = w_ref.shape[1]
        w_ref[...] = pack[:, :width]
        spot = jnp.broadcast_to(pack[:, width : width + 1], (64, 64))
        b_ref[...] = jnp.sum(jnp.where(row == col, spot, 0.0), axis=0, keepdims=True)


def swap(cells, axis, bit):
    return lax.ppermute(cells, axis, [(i, i ^ bit) for i in range(lax.axis_size(axis))])


def pair_swap(cells, first):
    count = lax.axis_size("space")
    pairs = [(i, i + 1) for i in range(first, count - 1, 2)]
    return lax.ppermute(cells, "space", pairs + [(j, i) for i, j in pairs])


def halo(own, edge, *ready):
    side, *ready = hold((swap(edge, "ysp", 1), *ready))
    cells = jnp.concatenate([own, side], axis=1)
    even = pair_swap(cells, 0)
    odd = pair_swap(cells, 1)
    return side, even, odd, *ready


def powers(axis, first):
    return [m for m in (1, 2, 4, 8, 16, 32, 64) if first <= m < lax.axis_size(axis)]


def cross(cells, axis, bit):
    pairs = [(2 * i + c, 2 * (i ^ bit) + 1 - c) for i in range(lax.axis_size(axis)) for c in range(2)]
    return lax.ppermute(cells, (axis, "ysp"), pairs)


def on_device(inputs, w_first, b_first, w_second, b_second, cotangent):
    nx, ny = inputs.shape[1], inputs.shape[2]
    own = inputs.reshape(nx, ny, ROWS, IN_L)
    edge = lax.dynamic_slice_in_dim(own, (1 - lax.axis_index("ysp")) * (ny - 2), 2, axis=1)
    side, even, odd = halo(own, edge)
    hbm = pl.BlockSpec(memory_space=pltpu.HBM)
    banded = call(
        banded_body,
        2000000000,
        [
            ((256, 9 * 256), BF),
            ((256, 9 * 384), BF),
            ((9, 384, 256), BF),
            ((9, 384, 128), BF),
            ((2, MID_L), F32),
        ],
        [
            pltpu.VMEM((64, W1_L), F32),
            pltpu.VMEM((64, W2_L), F32),
            pltpu.VMEM((2, C_MID), F32),
            pltpu.SemaphoreType.DMA((4,)),
        ],
        vmem=16 << 20,
        in_specs=[hbm] * 4,
    )(*[pltpu.with_memory_space_constraint(v, pltpu.HBM) for v in (w_first.T, w_second.T, b_first.reshape(1, C_MID), b_second.reshape(1, C_MID))])
    cot = cotangent.reshape(nx, ny, ROWS, MID_L)
    even, odd, cot, f1, f2, r2, r1, bias = hold((even, odd, cot, *banded))
    wide_in, act, y1, out, g2, edge = call(
        forward_body,
        4800000000,
        [
            ((nx + 4, ny + 4, ROWS, 256), BF),
            ((nx + 2, ny + 2, ROWS, 384), BF),
            ((nx + 2, ny + 2, ROWS, MID_L), F32),
            ((nx, ny, ROWS, MID_L), BF),
            ((nx, ny, ROWS, MID_L), BF),
            ((nx, 2, ROWS, MID_L), BF),
        ],
        [pltpu.VMEM(((nx + 2) * (ny + 1) * ROWS, MID_L), F32)],
    )(own, side, even, odd, f1, f2, bias, cot)
    keep2, send2 = call(
        second_weights_body, 1800000000, [((32, PACK2), F32), ((32, PACK2), BF)], [pltpu.VMEM((64, PACK2), F32)]
    )(act, g2)
    side, even, odd, keep2, send2, y1 = halo(g2, edge, keep2, send2, y1)
    got2 = cross(send2, "dp", 1)
    (slope,) = call(slope_body, 1600000000, [((nx + 2, ny + 2, ROWS, MID_L), F32)])(y1)
    odd, even, keep2, got2, slope = hold((odd, even, keep2, got2, slope))
    keep, send, g1 = call(
        backward_body,
        5600000000,
        [((64, PACK1), F32), ((64, PACK1), BF), ((nx, ny, ROWS, MID_L), BF)],
        [
            pltpu.VMEM((nx + 2, ny + 2, ROWS, 384), BF),
            pltpu.VMEM((64, PACK1), F32),
            pltpu.VMEM((32, PACK2), F32),
        ],
    )(g2, side, even, odd, r2, slope, wide_in, keep2, got2)
    total = hold((keep + swap(send, "ysp", 1).astype(F32)).astype(BF))
    sum1, sum2 = hold((total[:32], total[32:]))
    (wide_g,) = call(
        outer_body,
        1400000000,
        [((nx + 2, ny + 2, ROWS, 384), BF)],
        [pltpu.VMEM((nx + 4, ny + 4, ROWS, 384), BF)],
    )(g2, side, even, odd, r2, slope, g1)
    output = out.reshape(1, nx, ny, DEPTH * C_MID)
    along = [("space", m) for m in powers("space", 1)]
    stages1 = [("dp", m) for m in powers("dp", 1)] + along
    stages2 = [("dp", m) for m in powers("dp", 2)] + along
    for at, (one, two) in enumerate(zip(stages1, [*stages2, None])):
        got1 = cross(sum1, *one)
        got2 = cross(sum2, *(two or ("dp", 1)))
        if at == 0:
            got1, wide_g = hold((got1, wide_g))
            (d_in,) = call(input_grad_body, 1200000000, [((nx, ny, ROWS, IN_L), BF)])(wide_g, r1)
            input_grad = d_in.reshape(1, nx, ny, DEPTH * C_IN)
        if at == 2:
            got1, output = hold((got1, output))
        if at == 2:
            got1, input_grad = hold((got1, input_grad))
        sum1 = hold(sum1 + got1)
        if two:
            sum2 = hold(sum2 + got2)
    total = jnp.concatenate([sum2, got2, sum1], axis=0)
    gw2, gb2, gw1, gb1 = call(
        finish_body,
        1200000000,
        [((64, W2_L), F32), ((1, 64), F32), ((64, W1_L), F32), ((1, 64), F32)],
        [pltpu.VMEM((64, PACK2), F32), pltpu.VMEM((64, PACK1), F32)],
    )(total, swap(total, "ysp", 1))
    return (output, input_grad, gw1.T, gb1.reshape(64), gw2.T, gb2.reshape(64))


def solution(mesh):
    placed = P(("groups", "dp"), "space", "ysp", None)
    return jax.shard_map(
        on_device,
        mesh=mesh,
        in_specs=(placed, P(), P(), P(), P(), placed),
        out_specs=(placed, placed, P("groups", None), P("groups"), P("groups", None), P("groups")),
        check_vma=False,
    )
```
